128 devices in a mesh: dom: 128 (over x, y, z, core).
Axes of the slice: x: 4, y: 4, z: 4, core: 2. Of those that a mesh axis runs over, the one named last changes fastest.
Arguments:
- features: bfloat16 [524288, 128], P('dom'), may hold values from -6 to 6
- hubs: bfloat16 [8192, 128], P('dom'), may hold values from -6 to 6
- weight: bfloat16 [128, 128], replicated, may hold values from -0.5 to 0.5
- bias: float32 [128], replicated, may hold values from -3 to 3
- cotangent: bfloat16 [524288, 128], P('dom'), may hold values from -6 to 6
- tiles: bfloat16 [65536, 128, 128], P('dom'), may hold values from 0 to 0.049804688
- tile_blocks: int32 [65536, 2], P('dom'), may hold values from 0 to 95, as said below
- tile_count: int32 [128], P('dom'), may hold values from 96 to 512, as said below
- halo_send: int32 [128, 128, 32], P('dom'), may hold values from 0 to 4095
- replica_rows: int32 [128, 128, 32], P('dom'), may hold values from 0 to 63
Outputs:
- activations: bfloat16 [524288, 128], P('dom')
- saliency: float32 [524288, 128], P('dom')
- hub_saliency: float32 [8192, 128], P('dom')
The draws below stay inside these ranges and needn't reach their ends.
Inputs may be any that keep to these rules, and one draw needn't show every extreme that they name: `tile_blocks`: the first 96 tile slots of each partition name every column block of its extended table once; the others name any row and column blocks. `tile_count`: some partition has all 512 slots live.
All inputs are finite; a program needn't handle non-finite values.
Results may differ from the reference program's by a relative error of at most 0.0054.
Values may be sent and summed in bfloat16 or wider, within the bound.
No kernel may reach another device: no remote copies, remote signals or barrier semaphores. Data moves between devices by JAX's collectives and lax.ppermute only.
A program may use at most 128 MiB of HBM per device.

```python
import jax
import jax.numpy as jnp
from jax import lax

F = 128
HID = 128
BLK = 128
V_DEV = 4096
HUB_DEV = 64
S = 32
RS = 32
TILES_DEV = 512
VERTS = 524288
HUBS = 8192
ALL_TILES = 65536
EXT_BLOCKS = 96
N_DOM = 128


def draw_tile_blocks(key, part):

    def one_partition(subkey):
        key_cover, key_extra, key_rows = jax.random.split(subkey, 3)
        cover = jax.random.permutation(key_cover, EXT_BLOCKS).astype(jnp.int32)
        extra = jax.random.randint(key_extra, (TILES_DEV - EXT_BLOCKS,), 0, EXT_BLOCKS, dtype=jnp.int32)
        columns = jnp.concatenate([cover, extra])
        rows_drawn = jax.random.randint(key_rows, (TILES_DEV,), 0, V_DEV // BLK, dtype=jnp.int32)
        return jnp.stack([rows_drawn, columns], 1)
    subkeys = jax.random.split(jax.random.fold_in(key, 11), N_DOM)
    return jax.vmap(one_partition)(subkeys).reshape(N_DOM * TILES_DEV, 2).astype(jnp.int32)


def draw_tile_count(key, part):
    key_raw, key_busy = jax.random.split(jax.random.fold_in(key, 23))
    spread = TILES_DEV - EXT_BLOCKS
    raw_draw = jax.random.randint(key_raw, (N_DOM,), 0, spread + 1, dtype=jnp.int32)
    counts = EXT_BLOCKS + raw_draw * raw_draw // max(spread, 1)
    busiest = jax.random.randint(key_busy, (), 0, N_DOM, dtype=jnp.int32)
    chosen = jnp.arange(N_DOM, dtype=jnp.int32) == busiest
    return jnp.where(chosen, TILES_DEV, counts).astype(jnp.int32)


def plant(array, rng, least, largest):
    place = [jax.random.randint(jax.random.fold_in(rng, axis), (), 0, length) for axis, length in enumerate(array.shape)]
    widest = array.shape.index(max(array.shape))
    beside = place[:widest] + [(place[widest] + 1) % array.shape[widest]] + place[widest + 1:]
    return array.at[tuple(place)].set(least).at[tuple(beside)].set(largest)


def level_of(stream_key, shape, cuts, low, high):
    def one(position, shards_of):
        steps = jax.random.uniform(jax.random.fold_in(jax.random.fold_in(stream_key, 6), position), (shards_of,), jnp.float32, low / len(cuts), high / len(cuts))
        return jnp.repeat(jnp.exp(steps), shape[position] // shards_of).reshape((-1,) + (1,) * (len(shape) - position - 1))

    gain = one(*cuts[0])
    for cut in cuts[1:]:
        gain = gain * one(*cut)
    return gain


def noise(rng, extent, width, limit, shards=(), kind=jnp.bfloat16):
    loudness = level_of(rng, extent, shards, -0.22, 0.18) if shards else 1.0
    drawn = jax.random.normal(rng, extent, jnp.float32) * width * loudness
    return jnp.minimum(jnp.maximum(drawn, -limit), limit).astype(kind)


def setup_inputs(seed: int = 0) -> dict:
    key_of = jax.random.split(jax.random.key(seed), 11)
    features = noise(key_of[0], (VERTS, F), 1.0, 6.0, ((0, 128),))
    hubs = noise(key_of[1], (HUBS, F), 1.0, 6.0, ((0, 128),))
    weight = noise(key_of[2], (F, HID), F ** -0.5, 0.5)
    bias = noise(key_of[3], (HID,), 0.5, 3.0, (), jnp.float32)
    cotangent = noise(key_of[4], (VERTS, HID), 1.0, 6.0, ((0, 128),))
    tiles = jnp.clip(0.049804688 * jax.random.uniform(key_of[5], (ALL_TILES, BLK, BLK), jnp.float32) ** level_of(key_of[5], (ALL_TILES, BLK, BLK), ((0, 128),), -0.2, 0.2), 0.0, 0.049804688).astype(jnp.bfloat16)
    tile_blocks = draw_tile_blocks(jax.random.fold_in(key_of[10], 71), 0)
    tile_count = draw_tile_count(jax.random.fold_in(key_of[10], 71), 0)
    halo_send = plant(jax.random.randint(key_of[8], (N_DOM, N_DOM, S), 0, V_DEV), jax.random.fold_in(key_of[8], 1), 0, V_DEV - 1).astype(jnp.int32)
    replica_rows = plant(jax.random.randint(key_of[9], (N_DOM, N_DOM, RS), 0, HUB_DEV), jax.random.fold_in(key_of[9], 1), 0, HUB_DEV - 1).astype(jnp.int32)
    return dict(features=features, hubs=hubs, weight=weight, bias=bias, cotangent=cotangent, tiles=tiles, tile_blocks=tile_blocks, tile_count=tile_count, halo_send=halo_send, replica_rows=replica_rows)


def silu_slope(preact):
    sigmoid = jax.nn.sigmoid(preact)
    return sigmoid * (1.0 + preact * (1.0 - sigmoid))


def reference(features, hubs, weight, bias, cotangent, tiles, tile_blocks, tile_count, halo_send, replica_rows):
    grouped = features.reshape(N_DOM, V_DEV, F)
    masters = (jnp.arange(N_DOM, dtype=jnp.int32) * HUB_DEV)[None, :, None]
    hub_index = (replica_rows + masters).reshape(N_DOM, N_DOM * RS)
    tile_values = tiles.reshape(N_DOM, TILES_DEV, BLK, BLK)
    tile_places = tile_blocks.reshape(N_DOM, TILES_DEV, 2)
    upstream_all = cotangent.reshape(N_DOM, V_DEV, HID)
    owners = jnp.arange(N_DOM, dtype=jnp.int32)[:, None]
    positions = jnp.arange(TILES_DEV, dtype=jnp.int32)

    def one_part(totals, part_index):
        feature_grad, hub_grad = totals
        sources = halo_send[:, part_index, :]
        halo_rows = grouped[owners, sources].reshape(N_DOM * S, F)
        replica_index = hub_index[part_index]
        replicas = hubs[replica_index]
        ext_table = jnp.concatenate([grouped[part_index], halo_rows, replicas], 0).reshape(EXT_BLOCKS, BLK, F)
        values = tile_values[part_index].astype(jnp.float32)
        places = tile_places[part_index]
        active = (positions < tile_count[part_index])[:, None, None]
        product = jnp.einsum("tij,tjf->tif", values, ext_table[places[:, 1]].astype(jnp.float32))
        product = jnp.where(active, product, 0.0)
        summed = jnp.zeros((V_DEV // BLK, BLK, F), jnp.float32).at[places[:, 0]].add(product)
        aggregated = summed.reshape(V_DEV, F).astype(jnp.bfloat16)
        preact = jnp.dot(aggregated, weight, preferred_element_type=jnp.float32) + bias
        activation = jax.nn.silu(preact).astype(jnp.bfloat16)
        upstream = (upstream_all[part_index].astype(jnp.float32) * silu_slope(preact)).astype(jnp.bfloat16)
        back_rows = jnp.dot(upstream, weight.T, preferred_element_type=jnp.float32).astype(jnp.bfloat16)
        incoming = back_rows.reshape(V_DEV // BLK, BLK, F)[places[:, 0]].astype(jnp.float32)
        spread = jnp.einsum("tij,tif->tjf", values, incoming)
        spread = jnp.where(active, spread, 0.0)
        ext_grad = jnp.zeros((EXT_BLOCKS, BLK, F), jnp.float32).at[places[:, 1]].add(spread)
        ext_grad = ext_grad.reshape(EXT_BLOCKS * BLK, F)
        feature_grad = feature_grad.at[part_index].add(ext_grad[:V_DEV])
        halo_grad = ext_grad[V_DEV:V_DEV + N_DOM * S].reshape(N_DOM, S, F)
        feature_grad = feature_grad.at[owners, sources].add(halo_grad)
        hub_grad = hub_grad.at[replica_index].add(ext_grad[V_DEV + N_DOM * S:])
        return (feature_grad, hub_grad), activation

    initial = (jnp.zeros((N_DOM, V_DEV, F), jnp.float32), jnp.zeros((HUBS, F), jnp.float32))
    (feature_grad, hub_grad), activations = lax.scan(one_part, initial, jnp.arange(N_DOM, dtype=jnp.int32))
    return activations.reshape(VERTS, HID), feature_grad.reshape(VERTS, F), hub_grad
```

```python
import functools

import jax
import jax.numpy as jnp
from jax import lax
from jax.experimental import pallas as pl
from jax.experimental.pallas import tpu as pltpu
from jax.sharding import PartitionSpec as P

VMEM = pltpu.VMEM
SMEM = pltpu.SMEM
F32 = jnp.float32
BF16 = jnp.bfloat16
I32 = jnp.int32
UNROLL = 8
NT = (((1,), (1,)), ((), ()))


def whole(space):
    return pl.BlockSpec(memory_space=space)


def params(mib=None):
    return pltpu.CompilerParams(
        vmem_limit_bytes=None if mib is None else mib << 20
    )


def outgoing_kernel(send_ref, feat_ref, hub_ref, wanted_ref, out_ref, wide, stage):
    step = pl.program_id(0)
    parties = out_ref.shape[0]
    rows = send_ref.shape[1]
    half = hub_ref.shape[0] // 2

    @pl.when(step == 0)
    def _():
        wide[...] = feat_ref[...].astype(F32)

    halves = (hub_ref[:half, :], hub_ref[half:, :])
    repeat = feat_ref.shape[1] // wanted_ref.shape[1]

    @pl.loop(0, parties // 2)
    def _(pair):
        for side in range(2):
            q = pair * 2 + side
            for j in range(rows):
                row = send_ref[step * parties + q, j]
                stage[side, pl.ds(j, 1), :] = wide[pl.ds(row, 1), :]
            out_ref[q, 0:rows, :] = stage[side].astype(BF16)
            out_ref[q, rows : rows + half, :] = halves[side]
            names = wanted_ref[pl.ds(q, 1), :].astype(F32)
            names = jnp.concatenate([names] * repeat, axis=1)
            out_ref[q, rows + half :, :] = jnp.broadcast_to(
                names, (out_ref.shape[1] - rows - half, names.shape[1])
            ).astype(BF16)


def outgoing_rows(send, features, hubs, wanted):
    parties, rows = send.shape
    width = features.shape[1]
    half = hubs.shape[0] // 2
    total = rows + half + 8
    steps = 8
    chunk = parties // steps
    return pl.pallas_call(
        outgoing_kernel,
        name="outgoing_rows",
        grid=(steps,),
        in_specs=[
            whole(SMEM),
            pl.BlockSpec(features.shape, lambda i: (0, 0)),
            pl.BlockSpec(hubs.shape, lambda i: (0, 0)),
            pl.BlockSpec((chunk, wanted.shape[1]), lambda i: (i, 0)),
        ],
        out_specs=pl.BlockSpec((chunk, total, width), lambda i: (i, 0, 0)),
        out_shape=jax.ShapeDtypeStruct((parties, total, width), BF16),
        scratch_shapes=[VMEM(features.shape, F32), VMEM((2, rows, width), F32)],
        compiler_params=params(),
        cost_estimate=pl.CostEstimate(flops=0, bytes_accessed=30 << 20, transcendentals=0),
    )(send, features, hubs, wanted)


def unpack(entry):
    return entry & 1023, (entry >> 10) & 63, entry >> 16


def tile_loop(list_ref, kind, live, tiles_ref, ring, sems, body):
    depth = ring.shape[0]
    groups = (live + UNROLL - 1) // UNROLL

    def start(group):
        slot = group % depth
        for u in range(UNROLL):
            tile, _, _ = unpack(list_ref[kind, group * UNROLL + u])
            pltpu.make_async_copy(tiles_ref.at[tile], ring.at[slot, u], sems.at[slot]).start()

    for ahead in range(depth - 1):

        @pl.when(ahead < groups)
        def _():
            start(jnp.int32(ahead))

    @pl.loop(0, groups)
    def _(group):
        @pl.when(group + depth - 1 < groups)
        def _():
            start(group + depth - 1)

        slot = group % depth
        pltpu.make_async_copy(
            tiles_ref.at[pl.ds(0, UNROLL)], ring.at[slot], sems.at[slot]
        ).wait()
        for u in range(UNROLL):
            _, row, column = unpack(list_ref[kind, group * UNROLL + u])
            body(ring[slot, u], row, column)


def own_forward_kernel(count_ref, rows_ref, feat_ref, tiles_ref, sum_ref, list_ref, live_ref, ring, total, sems):
    blocks = feat_ref.shape[0]
    count = count_ref[0]
    total[...] = jnp.zeros_like(total)

    def classify(t, lives):
        row = rows_ref[t, 0]
        column = rows_ref[t, 1]
        kind = column // blocks
        entry = t | (row << 10) | (column << 16)
        place = jnp.where(kind == 0, lives[0], jnp.where(kind == 1, lives[1], lives[2]))
        list_ref[kind, place] = entry
        return tuple(lives[k] + (kind == k).astype(I32) for k in range(3))

    lives = lax.fori_loop(0, count, classify, (jnp.int32(0),) * 3)
    for k in range(3):
        live_ref[k] = lives[k]
        for u in range(UNROLL):
            list_ref[k, lives[k] + u] = jnp.int32((blocks << 10) | (3 * blocks << 16))

    def body(values, row, column):
        column = jnp.minimum(column, blocks - 1)
        total[row] += jnp.dot(values, feat_ref[column], preferred_element_type=F32)

    tile_loop(list_ref, 0, lives[0], tiles_ref, ring, sems, body)
    sum_ref[...] = total[:blocks]


def own_forward(count, places, features, tiles):
    tile = tiles.shape[1]
    blocks = features.shape[0] // tile
    width = features.shape[1]
    slots = tiles.shape[0] + UNROLL
    return pl.pallas_call(
        own_forward_kernel,
        name="own_forward",
        in_specs=[whole(SMEM), whole(SMEM), whole(VMEM), whole(pl.ANY)],
        out_specs=[whole(VMEM), whole(SMEM), whole(SMEM)],
        out_shape=[
            jax.ShapeDtypeStruct((blocks, tile, width), F32),
            jax.ShapeDtypeStruct((3, slots), I32),
            jax.ShapeDtypeStruct((3,), I32),
        ],
        scratch_shapes=[
            VMEM((4, UNROLL, tile, tile), BF16),
            VMEM((blocks + 1, tile, width), F32),
            pltpu.SemaphoreType.DMA((4,)),
        ],
        compiler_params=params(),
        cost_estimate=pl.CostEstimate(flops=10**9, bytes_accessed=40 << 20, transcendentals=0),
    )(count, places, features.reshape(blocks, tile, width), tiles)


def middle_kernel(
    list_ref, live_ref, side_ref, arrived_ref, other_ref, wanted_ref, start_ref, weight_ref, bias_ref,
    cot_ref, tiles_ref, act_ref, back_ref, grads_ref, ring, table, total, swapped, spread, sems,
):
    blocks, tile, width = start_ref.shape
    parties = arrived_ref.shape[0]
    rows = tile * blocks // parties
    group = tile // rows
    half = arrived_ref.shape[1] - rows - 8
    total[:blocks] = start_ref[...]
    weight = weight_ref[...]

    for b in range(blocks):
        table[b] = arrived_ref[b * group : (b + 1) * group, 0:rows, :].reshape(tile, width)

    def boundary_body(values, row, column):
        total[row] += jnp.dot(values, table[column - blocks], preferred_element_type=F32)

    tile_loop(list_ref, 1, live_ref[1], tiles_ref, ring, sems, boundary_body)

    side = side_ref[0]

    @pl.loop(0, blocks)
    def _(b):
        near = arrived_ref[pl.ds(b * group, group), rows : rows + half, :].reshape(group * half, width)
        far = other_ref[pl.ds(b * group, group), rows : rows + half, :].reshape(group * half, width)
        names = wanted_ref[b]
        lane = lax.broadcasted_iota(I32, (tile, group * half), 1)
        party = lax.broadcasted_iota(I32, (tile, group * half), 0) // rows
        is_far = ((names >= half).astype(I32) != side).astype(I32)
        target = jnp.where(names >= half, names - half, names) + party * half
        near_hot = jnp.where((lane == target) & (is_far == 0), 1.0, 0.0).astype(BF16)
        far_hot = jnp.where((lane == target) & (is_far == 1), 1.0, 0.0).astype(BF16)
        picked = jnp.dot(near_hot, near, preferred_element_type=F32)
        picked += jnp.dot(far_hot, far, preferred_element_type=F32)
        table[blocks + b] = picked.astype(BF16)

    tile_loop(list_ref, 2, live_ref[2], tiles_ref, ring, sems, boundary_body)

    @pl.loop(0, blocks)
    def _(b):
        preact = jnp.dot(total[b].astype(BF16), weight, preferred_element_type=F32) + bias_ref[...]
        sigmoid = 1.0 / (1.0 + jnp.exp(-preact))
        act_ref[b] = (preact * sigmoid).astype(BF16)
        slope = sigmoid * (1.0 + preact * (1.0 - sigmoid))
        upstream = (cot_ref[b].astype(F32) * slope).astype(BF16)
        swapped[b] = lax.dot_general(weight, upstream, NT, preferred_element_type=F32).astype(BF16)

    back_ref[...] = swapped[:blocks]
    spread[...] = jnp.zeros_like(spread)

    def backward_body(values, row, column):
        spread[column - blocks] += jnp.dot(swapped[row], values, preferred_element_type=F32)

    for kind in (1, 2):
        tile_loop(list_ref, kind, live_ref[kind], tiles_ref, ring, sems, backward_body)

    @pl.loop(0, blocks)
    def _(b):
        for part in range(2):
            out = jnp.transpose(spread[part * blocks + b]).astype(BF16)
            grads_ref[pl.ds(b * group, group), part * rows : (part + 1) * rows, :] = out.reshape(
                group, rows, width
            )


def middle(lists, lives, side, arrived, other, wanted, start, weight, bias, cotangent, tiles):
    blocks, tile, width = start.shape
    parties = arrived.shape[0]
    rows = tile * blocks // parties
    return pl.pallas_call(
        middle_kernel,
        name="middle",
        in_specs=[whole(SMEM)] * 3 + [whole(VMEM)] * 7 + [whole(pl.ANY)],
        out_specs=[whole(VMEM)] * 3,
        out_shape=[
            jax.ShapeDtypeStruct((blocks, tile, width), BF16),
            jax.ShapeDtypeStruct((blocks, width, tile), BF16),
            jax.ShapeDtypeStruct((parties, 2 * rows, width), BF16),
        ],
        scratch_shapes=[
            VMEM((4, UNROLL, tile, tile), BF16),
            VMEM((2 * blocks + 1, tile, width), BF16),
            VMEM((blocks + 1, tile, width), F32),
            VMEM((blocks + 1, width, tile), BF16),
            VMEM((2 * blocks + 1, width, tile), F32),
            pltpu.SemaphoreType.DMA((4,)),
        ],
        compiler_params=params(),
        cost_estimate=pl.CostEstimate(flops=4 * 10**9, bytes_accessed=60 << 20, transcendentals=10**6),
    )(
        lists, lives, side, arrived, other, wanted, start, weight, bias,
        cotangent.reshape(blocks, tile, width), tiles,
    )


def own_backward_kernel(list_ref, live_ref, back_ref, tiles_ref, own_ref, ring, swapped, spread, sems):
    blocks = back_ref.shape[0]
    swapped[:blocks] = back_ref[...]
    spread[...] = jnp.zeros_like(spread)

    def body(values, row, column):
        column = jnp.minimum(column, blocks)
        spread[column] += jnp.dot(swapped[row], values, preferred_element_type=F32)

    tile_loop(list_ref, 0, live_ref[0], tiles_ref, ring, sems, body)

    @pl.loop(0, blocks)
    def _(b):
        own_ref[b] = jnp.transpose(spread[b])


def own_backward(lists, lives, back, tiles):
    blocks, width, tile = back.shape
    return pl.pallas_call(
        own_backward_kernel,
        name="own_backward",
        in_specs=[whole(SMEM)] * 2 + [whole(VMEM), whole(pl.ANY)],
        out_specs=whole(VMEM),
        out_shape=jax.ShapeDtypeStruct((blocks, tile, width), F32),
        scratch_shapes=[
            VMEM((4, UNROLL, tile, tile), BF16),
            VMEM((blocks + 1, width, tile), BF16),
            VMEM((blocks + 1, width, tile), F32),
            pltpu.SemaphoreType.DMA((4,)),
        ],
        compiler_params=params(),
        cost_estimate=pl.CostEstimate(flops=10**9, bytes_accessed=40 << 20, transcendentals=0),
    )(lists, lives, back, tiles)


def returned_kernel(send_ref, own_ref, back_ref, names_ref, sal_ref, hub_ref, stage, chain1, chain2, chain3):
    parties, rows = send_ref.shape
    sal_ref[...] = own_ref[...]
    chains = (sal_ref, chain1, chain2, chain3)
    for chain in chains[1:]:
        chain[...] = jnp.zeros_like(chain)

    @pl.loop(0, parties)
    def _(q):
        stage[...] = back_ref[q, 0:rows, :].astype(F32)
        for j in range(rows):
            chain = chains[j % 4]
            row = send_ref[q, j]
            chain[pl.ds(row, 1), :] += stage[pl.ds(j, 1), :]

    sal_ref[...] += (chain1[...] + chain2[...]) + chain3[...]

    hubs, width = hub_ref.shape
    group = width // rows
    total = jnp.zeros((hubs, width), F32)
    lane = lax.broadcasted_iota(I32, (1, width), 1) // rows
    hub = lax.broadcasted_iota(I32, (hubs, width), 0).astype(F32)
    base = names_ref.shape[1] - 8
    for b in range(parties // group):
        names = jnp.zeros((1, width), F32)
        for i in range(group):
            row = names_ref[b * group + i, base : base + 1, :].astype(F32)
            names = jnp.where(lane == i, row, names)
        hot = jnp.where(hub == names, 1.0, 0.0).astype(BF16)
        grads = back_ref[b * group : (b + 1) * group, rows:, :].reshape(group * rows, width)
        total += jnp.dot(hot, grads, preferred_element_type=F32)
    hub_ref[...] = total


def returned_rows(send, own, returned, arrived, hubs):
    rows, width = own.shape
    return pl.pallas_call(
        returned_kernel,
        name="returned_rows",
        in_specs=[whole(SMEM)] + [whole(VMEM)] * 3,
        out_specs=[whole(VMEM)] * 2,
        out_shape=[
            jax.ShapeDtypeStruct((rows, width), F32),
            jax.ShapeDtypeStruct((hubs, width), F32),
        ],
        scratch_shapes=[VMEM((send.shape[1], width), F32)] + [VMEM((rows, width), F32)] * 3,
        compiler_params=params(),
        cost_estimate=pl.CostEstimate(flops=10**8, bytes_accessed=40 << 20, transcendentals=0),
    )(send, own, returned, arrived)


def body(
    features, hubs, weight, bias, cotangent, tiles, tile_blocks, tile_count, halo_send, replica_rows
):
    own_rows, width = features.shape
    tile = tiles.shape[1]
    blocks = own_rows // tile
    send = halo_send[0]
    wanted = replica_rows[0]
    parties = send.shape[0]
    side = (lax.axis_index("dom") % 2).astype(I32).reshape(1)

    outgoing = outgoing_rows(send, features, hubs, wanted)
    arrived = lax.all_to_all(outgoing, "dom", split_axis=0, concat_axis=0, tiled=True)
    other = lax.ppermute(arrived, "dom", [(i, i ^ 1) for i in range(parties)])
    start, lists, lives = own_forward(tile_count, tile_blocks, features, tiles)
    names = wanted.reshape(blocks, tile, 1)
    act, back, grads = middle(
        lists, lives, side, arrived, other, names, start, weight, bias.reshape(1, -1), cotangent, tiles
    )
    returned = lax.all_to_all(grads, "dom", split_axis=0, concat_axis=0, tiled=True)
    own = own_backward(lists, lives, back, tiles)
    saliency, hub_saliency = returned_rows(
        send, own.reshape(own_rows, width), returned, arrived, hubs.shape[0]
    )
    return act.reshape(own_rows, width), saliency, hub_saliency


def solution(mesh):
    placed = (
        P("dom", None),
        P("dom", None),
        P(),
        P(),
        P("dom", None),
        P("dom", None, None),
        P("dom", None),
        P("dom"),
        P("dom", None, None),
        P("dom", None, None),
    )
    return jax.shard_map(
        body,
        mesh=mesh,
        in_specs=placed,
        out_specs=(P("dom", None), P("dom", None), P("dom", None)),
        check_vma=False,
    )
```

```python
import functools

import jax
import jax.numpy as jnp
from jax import lax
from jax.experimental import pallas as pl
from jax.experimental.pallas import tpu as pltpu
from jax.sharding import PartitionSpec as P


VMEM = pltpu.VMEM
SMEM = pltpu.SMEM
F32 = jnp.float32
BF16 = jnp.bfloat16
I32 = jnp.int32
PAIRS = 4
NT = (((1,), (1,)), ((), ()))


def whole(space):
    return pl.BlockSpec(memory_space=space)


def params(mib):
    return pltpu.CompilerParams(vmem_limit_bytes=mib << 20)


def outgoing_kernel(send_ref, feat_ref, hub_ref, wanted_ref, out_ref, wide, stage, names):
    step = pl.program_id(0)
    chunk = out_ref.shape[0]
    rows = send_ref.shape[0]
    width = feat_ref.shape[1]
    half = hub_ref.shape[0] // 2

    @pl.when(step == 0)
    def _():
        wide[...] = feat_ref[...].astype(F32)
        tall = jnp.concatenate([wanted_ref[...].astype(F32)] * (width // rows), axis=0)
        names[...] = jnp.transpose(tall)

    halves = (hub_ref[:half, :], hub_ref[half:, :])

    @pl.loop(0, chunk // 2)
    def _(pair):
        for side in range(2):
            q = pair * 2 + side
            for j in range(rows):
                row = send_ref[j, step * chunk + q]
                stage[side, pl.ds(j, 1), :] = wide[pl.ds(row, 1), :]
        for side in range(2):
            q = pair * 2 + side
            out_ref[q, 0:rows, :] = stage[side].astype(BF16)
            out_ref[q, rows : rows + half, :] = halves[side]
            line = names[pl.ds(step * chunk + q, 1), :]
            out_ref[q, rows + half :, :] = jnp.broadcast_to(line, (8, width)).astype(BF16)


def outgoing_rows(send, features, hubs, wanted):
    rows, parties = send.shape
    width = features.shape[1]
    total = rows + hubs.shape[0] // 2 + 8
    steps = 4
    chunk = parties // steps
    return pl.pallas_call(
        outgoing_kernel,
        name="outgoing_rows",
        grid=(steps,),
        in_specs=[
            whole(SMEM),
            pl.BlockSpec(features.shape, lambda i: (0, 0)),
            pl.BlockSpec(hubs.shape, lambda i: (0, 0)),
            pl.BlockSpec(wanted.shape, lambda i: (0, 0)),
        ],
        out_specs=pl.BlockSpec((chunk, total, width), lambda i: (i, 0, 0)),
        out_shape=jax.ShapeDtypeStruct((parties, total, width), BF16),
        scratch_shapes=[
            VMEM(features.shape, F32),
            VMEM((2, rows, width), F32),
            VMEM((parties, width), F32),
        ],
        compiler_params=params(10),
        cost_estimate=pl.CostEstimate(flops=0, bytes_accessed=30 << 20, transcendentals=0),
    )(send, features, hubs, wanted)


def plan_kernel(blocks, count_ref, side_ref, places_ref, wanted_ref, list_ref, group_ref, hot_ref):
    slots = places_ref.shape[1]
    length = list_ref.shape[1]
    lanes = 128
    count = count_ref[0]
    row = places_ref[0:1, :]
    column = places_ref[1:2, :]
    slot = lax.broadcasted_iota(I32, (1, slots), 1)
    kind = jnp.where(column < blocks, 0, jnp.where(column < 2 * blocks, 1, 2))
    key = jnp.where(slot < count, kind * blocks + row, lanes - 1).astype(F32)
    entry = (slot | (row << 10) | (column << 16)).astype(F32)
    lines = jnp.concatenate([key, entry] + [jnp.zeros_like(key)] * 6, axis=0)
    tall = jnp.transpose(lines)
    key_tall, entry_tall = tall[:, 0:1], tall[:, 1:2]
    lane = lax.broadcasted_iota(I32, (1, lanes), 1)
    member = key_tall == lane.astype(F32)
    counts = jnp.sum(jnp.where(member, 1.0, 0.0), axis=0, keepdims=True)
    halves = jnp.where(lane < 3 * blocks, (counts.astype(I32) + 1) // 2, 0)
    before = jnp.where(
        lax.broadcasted_iota(I32, (lanes, lanes), 0) < lax.broadcasted_iota(I32, (lanes, lanes), 1), 1.0, 0.0
    ).astype(BF16)
    prefix = jnp.dot(
        jnp.broadcast_to(halves.astype(F32), (16, lanes)).astype(BF16), before, preferred_element_type=F32
    )[0:1, :].astype(I32)
    bucket = lane // blocks
    offset = prefix
    groups = jnp.zeros_like(lane)
    begun = jnp.zeros((1, 1), I32)
    passed = jnp.zeros((1, 1), I32)
    for k in range(3):
        pairs = jnp.sum(jnp.where(bucket == k, halves, 0), axis=1, keepdims=True)
        turns = (pairs + PAIRS - 1) // PAIRS
        offset = jnp.where(bucket == k, prefix + (begun * PAIRS - passed), offset)
        groups = jnp.where(lane == k, begun, groups)
        groups = jnp.where(lane == 3 + k, turns, groups)
        begun = begun + turns
        passed = passed + pairs
    group_ref[...] = groups
    first = jnp.sum(jnp.where(member, offset.astype(F32), 0.0), axis=1, keepdims=True)
    earlier = lax.broadcasted_iota(I32, (slots, slots), 1) < lax.broadcasted_iota(I32, (slots, slots), 0)
    index = jnp.sum(jnp.where((key_tall == key) & earlier, 1.0, 0.0), axis=1, keepdims=True)
    place = jnp.where(key_tall < 3 * blocks, 2.0 * first + index, -1.0)
    spare = float((blocks << 10) | (3 * blocks << 16))
    target = lax.broadcasted_iota(I32, (1, length), 1).astype(F32)
    placed = jnp.sum(jnp.where(place == target, entry_tall - spare, 0.0), axis=0, keepdims=True)
    list_ref[...] = (placed + spare).astype(I32)

    rows, parties = wanted_ref.shape
    group = hot_ref.shape[1] // rows
    half = hot_ref.shape[2] // 2 // group
    wanted = wanted_ref[...]
    member_of = lax.broadcasted_iota(I32, (rows, parties), 1) % group
    far = ((wanted >= half).astype(I32) != side_ref[0]).astype(I32)
    spot = jnp.where(wanted >= half, wanted - half, wanted) + member_of * half + far * (group * half)
    lane = lax.broadcasted_iota(I32, (rows, 2 * group * half), 1)
    for p in range(parties):
        hot = jnp.where(spot[:, p : p + 1] == lane, 1.0, 0.0)
        hot_ref[p // group, (p % group) * rows : (p % group + 1) * rows, :] = hot.astype(BF16)


def plan(count, side, places, wanted, blocks, tile):
    slots = places.shape[1]
    length = -(-(slots + 3 * blocks + 6 * PAIRS) // 128) * 128
    return pl.pallas_call(
        functools.partial(plan_kernel, blocks),
        name="plan",
        in_specs=[whole(SMEM), whole(SMEM), whole(VMEM), whole(VMEM)],
        out_specs=[whole(VMEM)] * 3,
        out_shape=[
            jax.ShapeDtypeStruct((1, length), I32),
            jax.ShapeDtypeStruct((1, 128), I32),
            jax.ShapeDtypeStruct((blocks, tile, 2 * tile), BF16),
        ],
        compiler_params=params(8),
        cost_estimate=pl.CostEstimate(flops=10**7, bytes_accessed=8 << 20, transcendentals=0),
    )(count, side, places, wanted)


def unpack(entry):
    return entry & 1023, (entry >> 10) & 63, entry >> 16


def start_group(list_ref, begin, turn, tiles_ref, store, sems, slot):
    for u in range(2 * PAIRS):
        tile, _, _ = unpack(list_ref[0, (begin + turn) * 2 * PAIRS + u])
        pltpu.make_async_copy(tiles_ref.at[tile], store.at[slot, u], sems.at[slot]).start()


def tile_loop(list_ref, begin, turns, tiles_ref, ring, sems, body):
    depth = ring.shape[0]
    for ahead in range(depth - 1):

        @pl.when(ahead < turns)
        def _():
            start_group(list_ref, begin, ahead, tiles_ref, ring, sems, ahead)

    @pl.loop(0, turns)
    def _(turn):
        later = turn + depth - 1

        @pl.when(later < turns)
        def _():
            start_group(list_ref, begin, later, tiles_ref, ring, sems, later % depth)

        slot = turn % depth
        pltpu.make_async_copy(
            tiles_ref.at[pl.ds(0, 2 * PAIRS)], ring.at[slot], sems.at[slot]
        ).wait()
        for u in range(PAIRS):
            _, row, left = unpack(list_ref[0, (begin + turn) * 2 * PAIRS + 2 * u])
            _, _, right = unpack(list_ref[0, (begin + turn) * 2 * PAIRS + 2 * u + 1])
            body(ring[slot, 2 * u], ring[slot, 2 * u + 1], row, left, right)


def forward_body(total, table, base):
    spare = table.shape[0] - 1

    def body(first, second, row, left, right):
        values = jnp.concatenate([first, second], axis=1)
        left = jnp.minimum(left - base, spare)
        right = jnp.minimum(right - base, spare)
        rows = jnp.concatenate([table[left], table[right]], axis=0)
        total[row] += jnp.dot(values, rows, preferred_element_type=F32)

    return body


def backward_body(spread, swapped, base):
    spare = spread.shape[0] - 1

    def body(first, second, row, left, right):
        tile = first.shape[1]
        values = jnp.concatenate([first, second], axis=1)
        product = jnp.dot(swapped[row], values, preferred_element_type=F32)
        spread[jnp.minimum(left - base, spare)] += product[:, :tile]
        spread[jnp.minimum(right - base, spare)] += product[:, tile:]

    return body


def own_forward_kernel(list_ref, group_ref, feat_ref, tiles_ref, sum_ref, ring, table, total, sems):
    blocks = feat_ref.shape[0]
    total[...] = jnp.zeros_like(total)
    table[:blocks] = feat_ref[...]
    table[blocks] = jnp.zeros(table.shape[1:], BF16)
    tile_loop(list_ref, group_ref[0, 0], group_ref[0, 3], tiles_ref, ring, sems, forward_body(total, table, 0))
    sum_ref[...] = total[:blocks]


def boundary_forward_kernel(list_ref, group_ref, near_ref, start_ref, tiles_ref, sum_ref, ring, table, total, sems):
    blocks, tile, width = start_ref.shape
    group = near_ref.shape[0] // blocks
    total[:blocks] = start_ref[...]
    for b in range(blocks):
        table[b] = near_ref[b * group : (b + 1) * group, 0 : tile // group, :].reshape(tile, width)
    table[blocks] = jnp.zeros(table.shape[1:], BF16)
    tile_loop(
        list_ref, group_ref[0, 1], group_ref[0, 4], tiles_ref, ring, sems, forward_body(total, table, blocks)
    )
    sum_ref[...] = total[:blocks]


def ring_scratch(tile):
    return [VMEM((4, 2 * PAIRS, tile, tile), BF16)]


def own_forward(lists, groups, features, tiles):
    tile = tiles.shape[1]
    blocks = features.shape[0] // tile
    width = features.shape[1]
    return pl.pallas_call(
        own_forward_kernel,
        name="own_forward",
        in_specs=[whole(SMEM), whole(SMEM), whole(VMEM), whole(pltpu.HBM)],
        out_specs=whole(VMEM),
        out_shape=jax.ShapeDtypeStruct((blocks, tile, width), F32),
        scratch_shapes=ring_scratch(tile)
        + [
            VMEM((blocks + 1, tile, width), BF16),
            VMEM((blocks + 1, tile, width), F32),
            pltpu.SemaphoreType.DMA((4,)),
        ],
        compiler_params=params(50),
        cost_estimate=pl.CostEstimate(flops=10**9, bytes_accessed=40 << 20, transcendentals=0),
    )(lists, groups, features.reshape(blocks, tile, width), tiles)


def boundary_forward(lists, groups, arrived, start, tiles):
    blocks, tile, width = start.shape
    return pl.pallas_call(
        boundary_forward_kernel,
        name="boundary_forward",
        in_specs=[
            whole(SMEM),
            whole(SMEM),
            whole(VMEM),
            whole(VMEM),
            whole(pltpu.HBM),
        ],
        out_specs=whole(VMEM),
        out_shape=jax.ShapeDtypeStruct(start.shape, F32),
        scratch_shapes=ring_scratch(tile)
        + [
            VMEM((blocks + 1, tile, width), BF16),
            VMEM((blocks + 1, tile, width), F32),
            pltpu.SemaphoreType.DMA((4,)),
        ],
        compiler_params=params(50),
        cost_estimate=pl.CostEstimate(flops=10**9, bytes_accessed=40 << 20, transcendentals=0),
    )(lists, groups, arrived, start, tiles)


def middle_kernel(
    list_ref, group_ref, near_ref, far_ref, hot_ref, start_ref, weight_ref, bias_ref,
    cot_ref, tiles_ref, act_ref, back_ref, grads_ref, ring, table, total, swapped, spread, sems,
):
    blocks, tile, width = start_ref.shape
    group = near_ref.shape[0] // blocks
    rows = tile // group
    total[:blocks] = start_ref[...]
    weight = weight_ref[...]

    @pl.loop(0, blocks // 4)
    def _(turn):
        for i in range(4):
            b = turn * 4 + i
            near = near_ref[pl.ds(b * group, group), rows : 2 * rows, :].reshape(tile, width)
            far = far_ref[pl.ds(b * group, group), rows : 2 * rows, :].reshape(tile, width)
            picked = jnp.dot(hot_ref[b], jnp.concatenate([near, far], axis=0), preferred_element_type=F32)
            table[b] = picked.astype(BF16)

    table[blocks] = jnp.zeros(table.shape[1:], BF16)
    tile_loop(
        list_ref, group_ref[0, 2], group_ref[0, 5], tiles_ref, ring, sems, forward_body(total, table, 2 * blocks)
    )

    @pl.loop(0, blocks // 4)
    def _(turn):
        for i in range(4):
            b = turn * 4 + i
            preact = jnp.dot(total[b].astype(BF16), weight, preferred_element_type=F32) + bias_ref[...]
            sigmoid = 0.5 * jnp.tanh(0.5 * preact) + 0.5
            act_ref[b] = (preact * sigmoid).astype(BF16)
            slope = sigmoid * (1.0 + preact * (1.0 - sigmoid))
            upstream = (cot_ref[b].astype(F32) * slope).astype(BF16)
            swapped[b] = lax.dot_general(weight, upstream, NT, preferred_element_type=F32).astype(BF16)

    back_ref[...] = swapped[:blocks]
    spread[...] = jnp.zeros_like(spread)
    tile_loop(
        list_ref,
        group_ref[0, 1],
        group_ref[0, 4] + group_ref[0, 5],
        tiles_ref,
        ring,
        sems,
        backward_body(spread, swapped, blocks),
    )

    @pl.loop(0, blocks // 2)
    def _(turn):
        for i in range(2):
            b = turn * 2 + i
            for part in range(2):
                out = jnp.transpose(spread[part * blocks + b].astype(BF16))
                grads_ref[pl.ds(b * group, group), part * rows : (part + 1) * rows, :] = out.reshape(
                    group, rows, width
                )


def middle(lists, groups, arrived, other, hot, start, weight, bias, cotangent, tiles):
    blocks, tile, width = start.shape
    parties = arrived.shape[0]
    rows = blocks * tile // parties
    return pl.pallas_call(
        middle_kernel,
        name="middle",
        in_specs=[whole(SMEM)] * 2
        + [whole(VMEM)] * 7
        + [whole(pltpu.HBM)],
        out_specs=[whole(VMEM)] * 3,
        out_shape=[
            jax.ShapeDtypeStruct((blocks, tile, width), BF16),
            jax.ShapeDtypeStruct((blocks, width, tile), BF16),
            jax.ShapeDtypeStruct((parties, 2 * rows, width), BF16),
        ],
        scratch_shapes=ring_scratch(tile)
        + [
            VMEM((blocks + 1, tile, width), BF16),
            VMEM((blocks + 1, tile, width), F32),
            VMEM((blocks + 1, width, tile), BF16),
            VMEM((2 * blocks + 1, width, tile), F32),
            pltpu.SemaphoreType.DMA((4,)),
        ],
        compiler_params=params(50),
        cost_estimate=pl.CostEstimate(flops=4 * 10**9, bytes_accessed=60 << 20, transcendentals=10**6),
    )(
        lists, groups, arrived, other, hot, start, weight, bias,
        cotangent.reshape(blocks, tile, width), tiles,
    )


def own_backward_kernel(
    list_ref, group_ref, back_ref, names_ref, tiles_ref, own_ref, hot_ref, ring, swapped, spread, sems
):
    blocks = back_ref.shape[0]
    swapped[:blocks] = back_ref[...]
    spread[...] = jnp.zeros_like(spread)
    tile_loop(
        list_ref, group_ref[0, 0], group_ref[0, 3], tiles_ref, ring, sems, backward_body(spread, swapped, 0)
    )

    @pl.loop(0, blocks // 2)
    def _(turn):
        for i in range(2):
            own_ref[turn * 2 + i] = jnp.transpose(spread[turn * 2 + i])

    parties, _, width = names_ref.shape
    group = parties // blocks
    rows = width // group
    names = names_ref[:, names_ref.shape[1] - 8, :].astype(F32)
    party = lax.broadcasted_iota(I32, names.shape, 0)
    lane = lax.broadcasted_iota(I32, names.shape, 1)
    names = jnp.where(lane // rows == party % group, names, 0.0).astype(BF16)
    block = lax.broadcasted_iota(I32, (blocks, parties), 0)
    gather = jnp.where(lax.broadcasted_iota(I32, (blocks, parties), 1) // group == block, 1.0, 0.0)
    lines = jnp.dot(gather.astype(BF16), names, preferred_element_type=F32)
    hub = lax.broadcasted_iota(I32, hot_ref.shape[1:], 0).astype(F32)
    for b in range(blocks):
        hot_ref[b] = jnp.where(hub == lines[b : b + 1, :], 1.0, 0.0).astype(BF16)


def own_backward(lists, groups, back, arrived, tiles, hubs):
    blocks, width, tile = back.shape
    return pl.pallas_call(
        own_backward_kernel,
        name="own_backward",
        in_specs=[whole(SMEM)] * 2
        + [whole(VMEM)] * 2
        + [whole(pltpu.HBM)],
        out_specs=[whole(VMEM)] * 2,
        out_shape=[
            jax.ShapeDtypeStruct((blocks, tile, width), F32),
            jax.ShapeDtypeStruct((blocks, hubs, width), BF16),
        ],
        scratch_shapes=ring_scratch(tile)
        + [
            VMEM((blocks + 1, width, tile), BF16),
            VMEM((blocks + 1, width, tile), F32),
            pltpu.SemaphoreType.DMA((4,)),
        ],
        compiler_params=params(50),
        cost_estimate=pl.CostEstimate(flops=10**9, bytes_accessed=40 << 20, transcendentals=0),
    )(lists, groups, back, arrived, tiles)


def returned_kernel(send_ref, own_ref, back_ref, hot_ref, sal_ref, hub_ref, stage, chain1, chain2, chain3):
    rows, parties = send_ref.shape
    blocks, _, width = hot_ref.shape
    group = parties // blocks
    sal_ref[...] = own_ref[...]
    chains = (sal_ref, chain1, chain2, chain3)
    for chain in chains[1:]:
        chain[...] = jnp.zeros_like(chain)

    @pl.loop(0, parties)
    def _(q):
        stage[...] = back_ref[q, 0:rows, :].astype(F32)
        for j in range(rows):
            chain = chains[j % 4]
            row = send_ref[j, q]
            chain[pl.ds(row, 1), :] += stage[pl.ds(j, 1), :]

    sal_ref[...] += (chain1[...] + chain2[...]) + chain3[...]

    total = jnp.zeros(hub_ref.shape, F32)
    for b in range(0, blocks, 2):
        grads = back_ref[b * group : (b + 2) * group, rows:, :].reshape(2 * group * rows, width)
        hot = jnp.concatenate([hot_ref[b], hot_ref[b + 1]], axis=1)
        total += jnp.dot(hot, grads, preferred_element_type=F32)
    hub_ref[...] = total


def returned_rows(send, own, returned, hot):
    rows, _ = send.shape
    own_rows, width = own.shape
    return pl.pallas_call(
        returned_kernel,
        name="returned_rows",
        in_specs=[
            whole(SMEM),
            whole(VMEM),
            whole(VMEM),
            whole(VMEM),
        ],
        out_specs=[whole(VMEM)] * 2,
        out_shape=[
            jax.ShapeDtypeStruct((own_rows, width), F32),
            jax.ShapeDtypeStruct((hot.shape[1], width), F32),
        ],
        scratch_shapes=[VMEM((rows, width), F32)] + [VMEM((own_rows, width), F32)] * 3,
        compiler_params=params(20),
        cost_estimate=pl.CostEstimate(flops=10**8, bytes_accessed=40 << 20, transcendentals=0),
    )(send, own, returned, hot)


def body(
    features, hubs, weight, bias, cotangent, tiles, tile_blocks, tile_count, halo_send, replica_rows
):
    own_rows, width = features.shape
    tile = tiles.shape[1]
    blocks = own_rows // tile
    send = halo_send[0].T
    wanted = replica_rows[0].T
    parties = send.shape[1]
    side = (lax.axis_index("dom") % 2).astype(I32).reshape(1)

    outgoing = outgoing_rows(send, features, hubs, wanted)
    arrived = lax.all_to_all(outgoing, "dom", split_axis=0, concat_axis=0, tiled=True)
    other = lax.ppermute(arrived, "dom", [(i, i ^ 1) for i in range(parties)])
    lists, groups, hot = plan(tile_count, side, tile_blocks.T, wanted, blocks, tile)
    start = own_forward(lists, groups, features, tiles)
    start = boundary_forward(lists, groups, arrived, start, tiles)
    act, back, grads = middle(lists, groups, arrived, other, hot, start, weight, bias.reshape(1, -1), cotangent, tiles)
    returned = lax.all_to_all(grads, "dom", split_axis=0, concat_axis=0, tiled=True)
    own, hub_hot = own_backward(lists, groups, back, arrived, tiles, hubs.shape[0])
    saliency, hub_saliency = returned_rows(send, own.reshape(own_rows, width), returned, hub_hot)
    return act.reshape(own_rows, width), saliency, hub_saliency


def solution(mesh):
    placed = (
        P("dom", None),
        P("dom", None),
        P(),
        P(),
        P("dom", None),
        P("dom", None, None),
        P("dom", None),
        P("dom"),
        P("dom", None, None),
        P("dom", None, None),
    )
    return jax.shard_map(
        body,
        mesh=mesh,
        in_specs=placed,
        out_specs=(P("dom", None), P("dom", None), P("dom", None)),
        check_vma=False,
    )
```

```python
import functools

import jax
import jax.numpy as jnp
from jax import lax
from jax.experimental import pallas as pl
from jax.experimental.pallas import tpu as pltpu
from jax.sharding import PartitionSpec as P


VMEM = pltpu.VMEM
SMEM = pltpu.SMEM
F32 = jnp.float32
BF16 = jnp.bfloat16
I32 = jnp.int32
PAIRS = 8
CHAINS = 6
NT = (((1,), (1,)), ((), ()))


def whole(space):
    return pl.BlockSpec(memory_space=space)


def params(mib):
    return pltpu.CompilerParams(vmem_limit_bytes=mib << 20)


def in_hbm(array):
    return pltpu.with_memory_space_constraint(array, pltpu.HBM)


def outgoing_kernel(send_ref, feat_ref, hub_ref, wanted_ref, out_ref, wide, stage, names):
    step = pl.program_id(0)
    chunk = out_ref.shape[0]
    rows = send_ref.shape[0]
    width = feat_ref.shape[1]
    half = hub_ref.shape[0] // 2

    @pl.when(step == 0)
    def _():
        wide[...] = feat_ref[...].astype(F32)
        tall = jnp.concatenate([wanted_ref[...].astype(F32)] * (width // rows), axis=0)
        names[...] = jnp.transpose(tall)

    halves = (hub_ref[:half, :], hub_ref[half:, :])

    @pl.loop(0, chunk // 2)
    def _(pair):
        for side in range(2):
            q = pair * 2 + side
            for j in range(rows):
                row = send_ref[j, step * chunk + q]
                stage[side, pl.ds(j, 1), :] = wide[pl.ds(row, 1), :]
        for side in range(2):
            q = pair * 2 + side
            out_ref[q, 0:rows, :] = stage[side].astype(BF16)
            out_ref[q, rows : rows + half, :] = halves[side]
            line = names[pl.ds(step * chunk + q, 1), :]
            out_ref[q, rows + half :, :] = jnp.broadcast_to(line, (8, width)).astype(BF16)


def outgoing_rows(send, features, hubs, wanted):
    rows, parties = send.shape
    width = features.shape[1]
    total = rows + hubs.shape[0] // 2 + 8
    steps = 4
    chunk = parties // steps
    return pl.pallas_call(
        outgoing_kernel,
        name="outgoing_rows",
        grid=(steps,),
        in_specs=[
            whole(SMEM),
            pl.BlockSpec(features.shape, lambda i: (0, 0)),
            pl.BlockSpec(hubs.shape, lambda i: (0, 0)),
            pl.BlockSpec(wanted.shape, lambda i: (0, 0)),
        ],
        out_specs=pl.BlockSpec((chunk, total, width), lambda i: (i, 0, 0)),
        out_shape=jax.ShapeDtypeStruct((parties, total, width), BF16),
        scratch_shapes=[
            VMEM(features.shape, F32),
            VMEM((2, rows, width), F32),
            VMEM((parties, width), F32),
        ],
        compiler_params=params(60),
        cost_estimate=pl.CostEstimate(flops=0, bytes_accessed=30 << 20, transcendentals=0),
    )(send, features, hubs, wanted)


def plan_kernel(blocks, count_ref, side_ref, places_ref, wanted_ref, list_ref, group_ref, hot_ref):
    slots = places_ref.shape[1]
    length = list_ref.shape[1]
    lanes = 128
    count = count_ref[0]
    row = places_ref[0:1, :]
    column = places_ref[1:2, :]
    slot = lax.broadcasted_iota(I32, (1, slots), 1)
    kind = jnp.where(column < blocks, 0, jnp.where(column < 2 * blocks, 1, 2))
    key = jnp.where(slot < count, kind * blocks + row, lanes - 1).astype(F32)
    entry = (slot | (row << 10) | (column << 16)).astype(F32)
    lines = jnp.concatenate([key, entry] + [jnp.zeros_like(key)] * 6, axis=0)
    tall = jnp.transpose(lines)
    key_tall, entry_tall = tall[:, 0:1], tall[:, 1:2]
    lane = lax.broadcasted_iota(I32, (1, lanes), 1)
    member = key_tall == lane.astype(F32)
    counts = jnp.sum(jnp.where(member, 1.0, 0.0), axis=0, keepdims=True)
    halves = jnp.where(lane < 3 * blocks, (counts.astype(I32) + 1) // 2, 0)
    before = jnp.where(
        lax.broadcasted_iota(I32, (lanes, lanes), 0) < lax.broadcasted_iota(I32, (lanes, lanes), 1), 1.0, 0.0
    ).astype(BF16)
    prefix = jnp.dot(
        jnp.broadcast_to(halves.astype(F32), (16, lanes)).astype(BF16), before, preferred_element_type=F32
    )[0:1, :].astype(I32)
    bucket = lane // blocks
    offset = prefix
    groups = jnp.zeros_like(lane)
    begun = jnp.zeros((1, 1), I32)
    passed = jnp.zeros((1, 1), I32)
    for k in range(3):
        pairs = jnp.sum(jnp.where(bucket == k, halves, 0), axis=1, keepdims=True)
        turns = (pairs + PAIRS - 1) // PAIRS
        offset = jnp.where(bucket == k, prefix + (begun * PAIRS - passed), offset)
        groups = jnp.where(lane == k, begun, groups)
        groups = jnp.where(lane == 3 + k, turns, groups)
        begun = begun + turns
        passed = passed + pairs
    group_ref[...] = groups
    first = jnp.sum(jnp.where(member, offset.astype(F32), 0.0), axis=1, keepdims=True)
    earlier = lax.broadcasted_iota(I32, (slots, slots), 1) < lax.broadcasted_iota(I32, (slots, slots), 0)
    index = jnp.sum(jnp.where((key_tall == key) & earlier, 1.0, 0.0), axis=1, keepdims=True)
    place = jnp.where(key_tall < 3 * blocks, 2.0 * first + index, -1.0)
    spare = float((blocks << 10) | (3 * blocks << 16))
    target = lax.broadcasted_iota(I32, (1, length), 1).astype(F32)
    placed = jnp.sum(jnp.where(place == target, entry_tall - spare, 0.0), axis=0, keepdims=True)
    list_ref[...] = (placed + spare).astype(I32)

    rows, parties = wanted_ref.shape
    group = hot_ref.shape[1] // rows
    half = hot_ref.shape[2] // 2 // group
    wanted = wanted_ref[...]
    member_of = lax.broadcasted_iota(I32, (rows, parties), 1) % group
    far = ((wanted >= half).astype(I32) != side_ref[0]).astype(I32)
    spot = jnp.where(wanted >= half, wanted - half, wanted) + member_of * half + far * (group * half)
    lane = lax.broadcasted_iota(I32, (rows, 2 * group * half), 1)
    for p in range(parties):
        hot = jnp.where(spot[:, p : p + 1] == lane, 1.0, 0.0)
        hot_ref[p // group, (p % group) * rows : (p % group + 1) * rows, :] = hot.astype(BF16)


def plan(count, side, places, wanted, blocks, tile):
    slots = places.shape[1]
    length = list_length(slots, blocks)
    return pl.pallas_call(
        functools.partial(plan_kernel, blocks),
        name="plan",
        in_specs=[whole(SMEM), whole(SMEM), whole(VMEM), whole(VMEM)],
        out_specs=[whole(VMEM)] * 3,
        out_shape=[
            jax.ShapeDtypeStruct((1, length), I32),
            jax.ShapeDtypeStruct((1, 128), I32),
            jax.ShapeDtypeStruct((blocks, tile, 2 * tile), BF16),
        ],
        compiler_params=params(60),
        cost_estimate=pl.CostEstimate(flops=10**7, bytes_accessed=8 << 20, transcendentals=0),
    )(count, side, places, wanted)


def unpack(entry):
    return entry & 1023, (entry >> 10) & 63, entry >> 16


def fetch_tiles(list_ref, begin, first, last, tiles_ref, store, sems):
    @pl.loop(first, last)
    def _(turn):
        for u in range(2 * PAIRS):
            tile, _, _ = unpack(list_ref[0, (begin + turn) * 2 * PAIRS + u])
            pltpu.make_async_copy(tiles_ref.at[tile], store.at[turn, u], sems.at[turn]).start()


def tile_loop(list_ref, begin, first, last, tiles_ref, store, sems, body):
    @pl.loop(first, last)
    def _(turn):
        if sems is not None:
            pltpu.make_async_copy(
                tiles_ref.at[pl.ds(0, 2 * PAIRS)], store.at[turn], sems.at[turn]
            ).wait()
        for u in range(PAIRS):
            place = (begin + turn) * 2 * PAIRS + 2 * u
            _, row, left = unpack(list_ref[0, place])
            _, _, right = unpack(list_ref[0, place + 1])
            body(store[turn, 2 * u], store[turn, 2 * u + 1], row, left, right)


def list_length(slots, blocks):
    return -(-(slots + 3 * blocks + 6 * PAIRS) // 128) * 128


def store_scratch(tiles, blocks):
    groups = (tiles.shape[0] + 3 * blocks) // (2 * PAIRS) + 4
    return [
        VMEM((groups, 2 * PAIRS) + tiles.shape[1:], BF16),
        pltpu.SemaphoreType.DMA((groups,)),
    ]


def forward_body(total, table, base):
    spare = table.shape[0] - 1

    def body(first, second, row, left, right):
        values = jnp.concatenate([first, second], axis=1)
        left = jnp.minimum(left - base, spare)
        right = jnp.minimum(right - base, spare)
        rows = jnp.concatenate([table[left], table[right]], axis=0)
        total[row] += jnp.dot(values, rows, preferred_element_type=F32)

    return body


def backward_body(spread, swapped, base):
    spare = spread.shape[0] - 1

    def body(first, second, row, left, right):
        tile = first.shape[1]
        values = jnp.concatenate([first, second], axis=1)
        product = jnp.dot(swapped[row], values, preferred_element_type=F32)
        spread[jnp.minimum(left - base, spare)] += product[:, :tile]
        spread[jnp.minimum(right - base, spare)] += product[:, tile:]

    return body


def own_forward_kernel(list_ref, group_ref, feat_ref, tiles_ref, sum_ref, table, total, store, sems):
    blocks = feat_ref.shape[0]
    begin, turns = group_ref[0, 0], group_ref[0, 3]
    fetch_tiles(list_ref, begin, 0, turns, tiles_ref, store, sems)
    total[...] = jnp.zeros_like(total)
    table[:blocks] = feat_ref[...]
    table[blocks] = jnp.zeros(table.shape[1:], BF16)
    tile_loop(list_ref, begin, 0, turns, tiles_ref, store, sems, forward_body(total, table, 0))
    sum_ref[...] = total[:blocks]


def own_forward(lists, groups, features, tiles):
    tile = tiles.shape[1]
    blocks = features.shape[0] // tile
    width = features.shape[1]
    return pl.pallas_call(
        own_forward_kernel,
        name="own_forward",
        in_specs=[whole(SMEM), whole(SMEM), whole(VMEM), whole(pltpu.HBM)],
        out_specs=whole(VMEM),
        out_shape=jax.ShapeDtypeStruct((blocks, tile, width), F32),
        scratch_shapes=[VMEM((blocks + 1, tile, width), BF16), VMEM((blocks + 1, tile, width), F32)]
        + store_scratch(tiles, blocks),
        compiler_params=params(50),
        cost_estimate=pl.CostEstimate(flops=10**9, bytes_accessed=40 << 20, transcendentals=0),
    )(lists, groups, features.reshape(blocks, tile, width), in_hbm(tiles))


def boundary_forward_kernel(
    list_ref, group_ref, near_ref, start_ref, tiles_ref, sum_ref, table, total, store, sems, start_sem
):
    blocks, tile, width = sum_ref.shape
    group = near_ref.shape[0] // blocks
    begin, turns = group_ref[0, 1], group_ref[0, 4]
    start_copy = pltpu.make_async_copy(start_ref, total.at[pl.ds(0, blocks)], start_sem)
    start_copy.start()
    fetch_tiles(list_ref, begin, 0, turns, tiles_ref, store, sems)
    for b in range(blocks):
        table[b] = near_ref[b * group : (b + 1) * group, 0 : tile // group, :].reshape(tile, width)
    table[blocks] = jnp.zeros(table.shape[1:], BF16)
    start_copy.wait()
    tile_loop(list_ref, begin, 0, turns, tiles_ref, store, sems, forward_body(total, table, blocks))
    sum_ref[...] = total[:blocks]


def boundary_forward(lists, groups, arrived, start, tiles):
    blocks, tile, width = start.shape
    return pl.pallas_call(
        boundary_forward_kernel,
        name="boundary_forward",
        in_specs=[whole(SMEM)] * 2 + [whole(VMEM), whole(pltpu.HBM), whole(pltpu.HBM)],
        out_specs=whole(VMEM),
        out_shape=jax.ShapeDtypeStruct(start.shape, F32),
        scratch_shapes=[VMEM((blocks + 1, tile, width), BF16), VMEM((blocks + 1, tile, width), F32)]
        + store_scratch(tiles, blocks)
        + [pltpu.SemaphoreType.DMA],
        compiler_params=params(40),
        cost_estimate=pl.CostEstimate(flops=10**9, bytes_accessed=40 << 20, transcendentals=0),
    )(lists, groups, arrived, in_hbm(start), in_hbm(tiles))


def middle_kernel(
    list_ref, group_ref, near_ref, far_ref, hot_ref, start_ref, weight_ref, bias_ref, cot_ref, tiles_ref,
    act_out, back_out, grads_ref, act_ref, table, total, swapped, spread, parcel, store, sems, out_sems,
):
    blocks, tile, width = act_ref.shape
    group = near_ref.shape[0] // blocks
    rows = tile // group
    weight = weight_ref[...]
    near_turns, hub_turns = group_ref[0, 4], group_ref[0, 5]
    fetch_tiles(list_ref, group_ref[0, 2], 0, hub_turns, tiles_ref, store, sems)
    fetch_tiles(list_ref, group_ref[0, 1] - hub_turns, hub_turns, hub_turns + near_turns, tiles_ref, store, sems)
    total[:blocks] = start_ref[...]

    @pl.loop(0, blocks // 4)
    def _(turn):
        for i in range(4):
            b = turn * 4 + i
            near = near_ref[pl.ds(b * group, group), rows : 2 * rows, :].reshape(tile, width)
            far = far_ref[pl.ds(b * group, group), rows : 2 * rows, :].reshape(tile, width)
            picked = jnp.dot(hot_ref[b], jnp.concatenate([near, far], axis=0), preferred_element_type=F32)
            table[b] = picked.astype(BF16)

    table[blocks] = jnp.zeros(table.shape[1:], BF16)
    tile_loop(
        list_ref, group_ref[0, 2], 0, hub_turns, tiles_ref, store, sems, forward_body(total, table, 2 * blocks)
    )

    @pl.loop(0, blocks // 4)
    def _(turn):
        for i in range(4):
            b = turn * 4 + i
            preact = jnp.dot(total[b].astype(BF16), weight, preferred_element_type=F32) + bias_ref[...]
            sigmoid = 0.5 * jnp.tanh(0.5 * preact) + 0.5
            act_ref[b] = (preact * sigmoid).astype(BF16)
            slope = sigmoid * (1.0 + preact * (1.0 - sigmoid))
            upstream = (cot_ref[b].astype(F32) * slope).astype(BF16)
            swapped[b] = lax.dot_general(weight, upstream, NT, preferred_element_type=F32).astype(BF16)

    results = (
        pltpu.make_async_copy(act_ref, act_out, out_sems.at[blocks // 2]),
        pltpu.make_async_copy(swapped.at[pl.ds(0, blocks)], back_out, out_sems.at[blocks // 2 + 1]),
    )
    for result in results:
        result.start()
    spread[...] = jnp.zeros_like(spread)
    add = backward_body(spread, swapped, blocks)
    tile_loop(list_ref, group_ref[0, 2], 0, hub_turns, tiles_ref, store, None, add)
    tile_loop(
        list_ref, group_ref[0, 1] - hub_turns, hub_turns, hub_turns + near_turns, tiles_ref, store, sems, add
    )

    chunk = 2 * group

    def send(turn):
        return pltpu.make_async_copy(
            parcel.at[pl.ds(turn * chunk, chunk)], grads_ref.at[pl.ds(turn * chunk, chunk)], out_sems.at[turn]
        )

    @pl.loop(0, blocks // 2)
    def _(turn):
        for i in range(2):
            b = turn * 2 + i
            for part in range(2):
                out = jnp.transpose(spread[part * blocks + b].astype(BF16))
                parcel[pl.ds(b * group, group), part * rows : (part + 1) * rows, :] = out.reshape(
                    group, rows, width
                )
        send(turn).start()

    @pl.loop(0, blocks // 2)
    def _(turn):
        send(turn).wait()

    for result in results:
        result.wait()


def middle(lists, groups, arrived, other, hot, start, weight, bias, cotangent, tiles):
    blocks, tile, width = start.shape
    parties = arrived.shape[0]
    rows = blocks * tile // parties
    return pl.pallas_call(
        middle_kernel,
        name="middle",
        in_specs=[whole(SMEM)] * 2
        + [whole(VMEM)] * 7
        + [whole(pltpu.HBM)],
        out_specs=[whole(pltpu.HBM)] * 3,
        out_shape=[
            pltpu.HBM((blocks, tile, width), BF16),
            pltpu.HBM((blocks, width, tile), BF16),
            pltpu.HBM((parties, 2 * rows, width), BF16),
        ],
        scratch_shapes=[
            VMEM((blocks, tile, width), BF16),
            VMEM((blocks + 1, tile, width), BF16),
            VMEM((blocks + 1, tile, width), F32),
            VMEM((blocks + 1, width, tile), BF16),
            VMEM((2 * blocks + 1, width, tile), F32),
            VMEM((parties, 2 * rows, width), BF16),
        ]
        + store_scratch(tiles, blocks)
        + [pltpu.SemaphoreType.DMA((blocks // 2 + 2,))],
        compiler_params=params(42),
        cost_estimate=pl.CostEstimate(flops=4 * 10**9, bytes_accessed=60 << 20, transcendentals=10**6),
    )(
        lists, groups, arrived, other, hot, start, weight, bias, cotangent.reshape(blocks, tile, width), in_hbm(tiles)
    )


def own_backward_kernel(
    list_ref, group_ref, back_ref, names_ref, tiles_ref, own_ref, hot_ref, swapped, spread, store, sems, back_sem
):
    blocks = back_ref.shape[0]
    begin, turns = group_ref[0, 0], group_ref[0, 3]
    back_copy = pltpu.make_async_copy(back_ref, swapped.at[pl.ds(0, blocks)], back_sem)
    back_copy.start()
    fetch_tiles(list_ref, begin, 0, turns, tiles_ref, store, sems)
    spread[...] = jnp.zeros_like(spread)
    back_copy.wait()
    tile_loop(list_ref, begin, 0, turns, tiles_ref, store, sems, backward_body(spread, swapped, 0))

    @pl.loop(0, blocks // 2)
    def _(turn):
        for i in range(2):
            own_ref[turn * 2 + i] = jnp.transpose(spread[turn * 2 + i])

    parties, total, width = names_ref.shape
    group = parties // blocks
    rows = width // group
    names = names_ref[:, total - 8, :].astype(F32)
    party = lax.broadcasted_iota(I32, names.shape, 0)
    lane = lax.broadcasted_iota(I32, names.shape, 1)
    names = jnp.where(lane // rows == party % group, names, 0.0).astype(BF16)
    block = lax.broadcasted_iota(I32, (blocks, parties), 0)
    gather = jnp.where(lax.broadcasted_iota(I32, (blocks, parties), 1) // group == block, 1.0, 0.0)
    lines = jnp.dot(gather.astype(BF16), names, preferred_element_type=F32)
    hub = lax.broadcasted_iota(I32, hot_ref.shape[1:], 0).astype(F32)
    for b in range(blocks):
        hot_ref[b] = jnp.where(hub == lines[b : b + 1, :], 1.0, 0.0).astype(BF16)


def own_backward(lists, groups, back, arrived, tiles, hubs):
    blocks, width, tile = back.shape
    return pl.pallas_call(
        own_backward_kernel,
        name="own_backward",
        in_specs=[whole(SMEM)] * 2 + [whole(pltpu.HBM), whole(VMEM), whole(pltpu.HBM)],
        out_specs=[whole(VMEM)] * 2,
        out_shape=[
            jax.ShapeDtypeStruct((blocks, tile, width), F32),
            jax.ShapeDtypeStruct((blocks, hubs, width), BF16),
        ],
        scratch_shapes=[VMEM((blocks + 1, width, tile), BF16), VMEM((blocks + 1, width, tile), F32)]
        + store_scratch(tiles, blocks)
        + [pltpu.SemaphoreType.DMA],
        compiler_params=params(50),
        cost_estimate=pl.CostEstimate(flops=10**9, bytes_accessed=40 << 20, transcendentals=0),
    )(lists, groups, in_hbm(back), arrived, in_hbm(tiles))


def returned_kernel(send_ref, own_ref, back_ref, hot_ref, sal_ref, hub_ref, stage, hot, chains, sems):
    rows, parties = send_ref.shape
    blocks, _, width = hot_ref.shape
    group = parties // blocks
    own_copy = pltpu.make_async_copy(own_ref, sal_ref, sems.at[0])
    hot_copy = pltpu.make_async_copy(hot_ref, hot, sems.at[1])
    own_copy.start()
    hot_copy.start()
    for chain in chains:
        chain[...] = jnp.zeros_like(chain)
    own_copy.wait()
    sums = (sal_ref,) + tuple(chains)

    @pl.loop(0, parties)
    def _(q):
        stage[...] = back_ref[q, 0:rows, :].astype(F32)
        for j in range(rows):
            chain = sums[j % len(sums)]
            row = send_ref[j, q]
            chain[pl.ds(row, 1), :] += stage[pl.ds(j, 1), :]

    total = sal_ref[...]
    for chain in chains:
        total = total + chain[...]
    sal_ref[...] = total

    hot_copy.wait()
    total = jnp.zeros(hub_ref.shape, F32)
    for b in range(0, blocks, 2):
        grads = back_ref[b * group : (b + 2) * group, rows:, :].reshape(2 * group * rows, width)
        pair = jnp.concatenate([hot[b], hot[b + 1]], axis=1)
        total += jnp.dot(pair, grads, preferred_element_type=F32)
    hub_ref[...] = total


def returned_rows(send, own, returned, hot):
    rows, _ = send.shape
    own_rows, width = own.shape
    return pl.pallas_call(
        returned_kernel,
        name="returned_rows",
        in_specs=[whole(SMEM), whole(pltpu.HBM), whole(VMEM), whole(pltpu.HBM)],
        out_specs=[whole(VMEM)] * 2,
        out_shape=[
            jax.ShapeDtypeStruct((own_rows, width), F32),
            jax.ShapeDtypeStruct((hot.shape[1], width), F32),
        ],
        scratch_shapes=[
            VMEM((rows, width), F32),
            VMEM(hot.shape, BF16),
            [VMEM((own_rows, width), F32)] * (CHAINS - 1),
            pltpu.SemaphoreType.DMA((2,)),
        ],
        compiler_params=params(32),
        cost_estimate=pl.CostEstimate(flops=10**8, bytes_accessed=40 << 20, transcendentals=0),
    )(send, in_hbm(own), returned, in_hbm(hot))


def body(
    features, hubs, weight, bias, cotangent, tiles, tile_blocks, tile_count, halo_send, replica_rows
):
    own_rows, width = features.shape
    tile = tiles.shape[1]
    blocks = own_rows // tile
    send = halo_send[0].T
    wanted = replica_rows[0].T
    parties = send.shape[1]
    side = (lax.axis_index("dom") % 2).astype(I32).reshape(1)

    pairs = [(i, i ^ 1) for i in range(parties)]

    outgoing = outgoing_rows(send, features, hubs, wanted)
    arrived = lax.all_to_all(outgoing, "dom", split_axis=0, concat_axis=0, tiled=True)
    lists, groups, hot = plan(tile_count, side, tile_blocks.T, wanted, blocks, tile)
    start = own_forward(lists, groups, features, tiles)
    other = lax.ppermute(arrived, "dom", pairs)
    start = boundary_forward(lists, groups, arrived, start, tiles)
    act, back, grads = middle(lists, groups, arrived, other, hot, start, weight, bias.reshape(1, -1), cotangent, tiles)
    returned = lax.all_to_all(grads, "dom", split_axis=0, concat_axis=0, tiled=True)
    own, hub_hot = own_backward(lists, groups, back, arrived, tiles, hubs.shape[0])
    saliency, hub_saliency = returned_rows(send, own.reshape(own_rows, width), returned, hub_hot)
    return act.reshape(own_rows, width), saliency, hub_saliency


def solution(mesh):
    placed = (
        P("dom", None),
        P("dom", None),
        P(),
        P(),
        P("dom", None),
        P("dom", None, None),
        P("dom", None),
        P("dom"),
        P("dom", None, None),
        P("dom", None, None),
    )
    return jax.shard_map(
        body,
        mesh=mesh,
        in_specs=placed,
        out_specs=(P("dom", None), P("dom", None), P("dom", None)),
        check_vma=False,
    )
```

```python
import functools

import jax
import jax.numpy as jnp
from jax import lax
from jax.experimental import pallas as pl
from jax.experimental.pallas import tpu as pltpu
from jax.sharding import PartitionSpec as P


VMEM = pltpu.VMEM
SMEM = pltpu.SMEM
F32 = jnp.float32
BF16 = jnp.bfloat16
I32 = jnp.int32
PAIRS = 8
CHAINS = 4
NT = (((1,), (1,)), ((), ()))


def whole(space):
    return pl.BlockSpec(memory_space=space)


def params(mib):
    return pltpu.CompilerParams(vmem_limit_bytes=mib << 20)


def in_hbm(array):
    return pltpu.with_memory_space_constraint(array, pltpu.HBM)


def outgoing_kernel(send_ref, feat_ref, hub_ref, wanted_ref, out_ref, wide, stage, names, parcel, sems):
    rows, parties = send_ref.shape
    width = feat_ref.shape[1]
    half = hub_ref.shape[0] // 2
    wide[...] = feat_ref[...].astype(F32)
    tall = jnp.concatenate([wanted_ref[...].astype(F32)] * (width // rows), axis=0)
    names[...] = jnp.transpose(tall)

    @pl.loop(0, rows)
    def _(j):
        for q in range(parties):
            stage[q, pl.ds(j, 1), :] = wide[pl.ds(send_ref[j, q], 1), :]

    halves = (hub_ref[:half, :], hub_ref[half:, :])
    turns = sems.shape[0]
    chunk = parties // turns

    def send(turn):
        part = pl.ds(turn * chunk, chunk)
        return pltpu.make_async_copy(parcel.at[part], out_ref.at[part], sems.at[turn])

    @pl.loop(0, turns)
    def _(turn):
        for i in range(chunk):
            q = turn * chunk + i
            parcel[q, 0:rows, :] = stage[q].astype(BF16)
            parcel[q, rows : rows + half, :] = halves[i % 2]
            line = names[pl.ds(q, 1), :]
            parcel[q, rows + half :, :] = jnp.broadcast_to(line, (8, width)).astype(BF16)
        send(turn).start()

    @pl.loop(0, turns)
    def _(turn):
        send(turn).wait()


def outgoing_rows(send, features, hubs, wanted):
    rows, parties = send.shape
    width = features.shape[1]
    total = rows + hubs.shape[0] // 2 + 8
    return pl.pallas_call(
        outgoing_kernel,
        name="outgoing_rows",
        in_specs=[whole(SMEM)] + [whole(VMEM)] * 3,
        out_specs=whole(pltpu.HBM),
        out_shape=pltpu.HBM((parties, total, width), BF16),
        scratch_shapes=[
            VMEM(features.shape, F32),
            VMEM((parties, rows, width), F32),
            VMEM((parties, width), F32),
            VMEM((parties, total, width), BF16),
            pltpu.SemaphoreType.DMA((16,)),
        ],
        compiler_params=params(60),
        cost_estimate=pl.CostEstimate(flops=0, bytes_accessed=30 << 20, transcendentals=0),
    )(send, features, hubs, wanted)


def plan_kernel(blocks, count_ref, side_ref, places_ref, wanted_ref, list_ref, group_ref, hot_ref):
    slots = places_ref.shape[1]
    length = list_ref.shape[1]
    lanes = 128
    count = count_ref[0]
    row = places_ref[0:1, :]
    column = places_ref[1:2, :]
    slot = lax.broadcasted_iota(I32, (1, slots), 1)
    kind = jnp.where(column < blocks, 0, jnp.where(column < 2 * blocks, 1, 2))
    key = jnp.where(slot < count, kind * blocks + row, lanes - 1).astype(F32)
    entry = (slot | (row << 10) | (column << 16)).astype(F32)
    lines = jnp.concatenate([key, entry] + [jnp.zeros_like(key)] * 6, axis=0)
    tall = jnp.transpose(lines)
    key_tall, entry_tall = tall[:, 0:1], tall[:, 1:2]
    lane = lax.broadcasted_iota(I32, (1, lanes), 1)
    member = key_tall == lane.astype(F32)
    counts = jnp.sum(jnp.where(member, 1.0, 0.0), axis=0, keepdims=True)
    halves = jnp.where(lane < 3 * blocks, (counts.astype(I32) + 1) // 2, 0)
    before = jnp.where(
        lax.broadcasted_iota(I32, (lanes, lanes), 0) < lax.broadcasted_iota(I32, (lanes, lanes), 1), 1.0, 0.0
    ).astype(BF16)
    prefix = jnp.dot(
        jnp.broadcast_to(halves.astype(F32), (16, lanes)).astype(BF16), before, preferred_element_type=F32
    )[0:1, :].astype(I32)
    bucket = lane // blocks
    offset = prefix
    groups = jnp.zeros_like(lane)
    begun = jnp.zeros((1, 1), I32)
    passed = jnp.zeros((1, 1), I32)
    for k in range(3):
        pairs = jnp.sum(jnp.where(bucket == k, halves, 0), axis=1, keepdims=True)
        turns = (pairs + PAIRS - 1) // PAIRS
        offset = jnp.where(bucket == k, prefix + (begun * PAIRS - passed), offset)
        groups = jnp.where(lane == k, begun, groups)
        groups = jnp.where(lane == 3 + k, turns, groups)
        begun = begun + turns
        passed = passed + pairs
    group_ref[...] = groups
    first = jnp.sum(jnp.where(member, offset.astype(F32), 0.0), axis=1, keepdims=True)
    earlier = lax.broadcasted_iota(I32, (slots, slots), 1) < lax.broadcasted_iota(I32, (slots, slots), 0)
    index = jnp.sum(jnp.where((key_tall == key) & earlier, 1.0, 0.0), axis=1, keepdims=True)
    place = jnp.where(key_tall < 3 * blocks, 2.0 * first + index, -1.0)
    spare = float((blocks << 10) | (3 * blocks << 16))
    target = lax.broadcasted_iota(I32, (1, length), 1).astype(F32)
    placed = jnp.sum(jnp.where(place == target, entry_tall - spare, 0.0), axis=0, keepdims=True)
    list_ref[...] = (placed + spare).astype(I32)

    rows, parties = wanted_ref.shape
    group = hot_ref.shape[1] // rows
    half = hot_ref.shape[2] // 2 // group
    wanted = wanted_ref[...]
    member_of = lax.broadcasted_iota(I32, (rows, parties), 1) % group
    far = ((wanted >= half).astype(I32) != side_ref[0]).astype(I32)
    spot = jnp.where(wanted >= half, wanted - half, wanted) + member_of * half + far * (group * half)
    lane = lax.broadcasted_iota(I32, (rows, 2 * group * half), 1)
    for p in range(parties):
        hot = jnp.where(spot[:, p : p + 1] == lane, 1.0, 0.0)
        hot_ref[p // group, (p % group) * rows : (p % group + 1) * rows, :] = hot.astype(BF16)


def plan(count, side, places, wanted, blocks, tile):
    slots = places.shape[1]
    length = list_length(slots, blocks)
    return pl.pallas_call(
        functools.partial(plan_kernel, blocks),
        name="plan",
        in_specs=[whole(SMEM), whole(SMEM), whole(VMEM), whole(VMEM)],
        out_specs=[whole(VMEM)] * 3,
        out_shape=[
            jax.ShapeDtypeStruct((1, length), I32),
            jax.ShapeDtypeStruct((1, 128), I32),
            jax.ShapeDtypeStruct((blocks, tile, 2 * tile), BF16),
        ],
        compiler_params=params(60),
        cost_estimate=pl.CostEstimate(flops=10**7, bytes_accessed=8 << 20, transcendentals=0),
    )(count, side, places, wanted)


def unpack(entry):
    return entry & 1023, (entry >> 10) & 63, entry >> 16


def fetch_tiles(list_ref, begin, first, last, tiles_ref, store, sems):
    @pl.loop(first, last)
    def _(turn):
        for u in range(2 * PAIRS):
            tile, _, _ = unpack(list_ref[0, (begin + turn) * 2 * PAIRS + u])
            pltpu.make_async_copy(tiles_ref.at[tile], store.at[turn, u], sems.at[turn]).start()


def tile_loop(list_ref, begin, first, last, tiles_ref, store, sems, body):
    @pl.loop(first, last)
    def _(turn):
        if sems is not None:
            pltpu.make_async_copy(
                tiles_ref.at[pl.ds(0, 2 * PAIRS)], store.at[turn], sems.at[turn]
            ).wait()
        for u in range(PAIRS):
            place = (begin + turn) * 2 * PAIRS + 2 * u
            _, row, left = unpack(list_ref[0, place])
            _, _, right = unpack(list_ref[0, place + 1])
            body(store[turn, 2 * u], store[turn, 2 * u + 1], row, left, right)


def list_length(slots, blocks):
    return -(-(slots + 3 * blocks + 6 * PAIRS) // 128) * 128


def store_scratch(tiles, blocks):
    groups = (tiles.shape[0] + 3 * blocks) // (2 * PAIRS) + 4
    return [
        VMEM((groups, 2 * PAIRS) + tiles.shape[1:], BF16),
        pltpu.SemaphoreType.DMA((groups,)),
    ]


def forward_body(total, table, base):
    spare = table.shape[0] - 1

    def body(first, second, row, left, right):
        values = jnp.concatenate([first, second], axis=1)
        left = jnp.minimum(left - base, spare)
        right = jnp.minimum(right - base, spare)
        rows = jnp.concatenate([table[left], table[right]], axis=0)
        total[row] += jnp.dot(values, rows, preferred_element_type=F32)

    return body


def backward_body(spread, swapped, base):
    spare = spread.shape[0] - 1

    def body(first, second, row, left, right):
        tile = first.shape[1]
        values = jnp.concatenate([first, second], axis=1)
        product = jnp.dot(swapped[row], values, preferred_element_type=F32)
        spread[jnp.minimum(left - base, spare)] += product[:, :tile]
        spread[jnp.minimum(right - base, spare)] += product[:, tile:]

    return body


def own_forward_kernel(list_ref, group_ref, feat_ref, tiles_ref, sum_ref, table, total, store, sems):
    blocks = feat_ref.shape[0]
    begin, turns = group_ref[0, 0], group_ref[0, 3]
    fetch_tiles(list_ref, begin, 0, turns, tiles_ref, store, sems)
    total[...] = jnp.zeros_like(total)
    table[:blocks] = feat_ref[...]
    table[blocks] = jnp.zeros(table.shape[1:], BF16)
    tile_loop(list_ref, begin, 0, turns, tiles_ref, store, sems, forward_body(total, table, 0))
    sum_ref[...] = total[:blocks]


def own_forward(lists, groups, features, tiles):
    tile = tiles.shape[1]
    blocks = features.shape[0] // tile
    width = features.shape[1]
    return pl.pallas_call(
        own_forward_kernel,
        name="own_forward",
        in_specs=[whole(SMEM), whole(SMEM), whole(VMEM), whole(pltpu.HBM)],
        out_specs=whole(VMEM),
        out_shape=jax.ShapeDtypeStruct((blocks, tile, width), F32),
        scratch_shapes=[VMEM((blocks + 1, tile, width), BF16), VMEM((blocks + 1, tile, width), F32)]
        + store_scratch(tiles, blocks),
        compiler_params=params(50),
        cost_estimate=pl.CostEstimate(flops=10**9, bytes_accessed=40 << 20, transcendentals=0),
    )(lists, groups, features.reshape(blocks, tile, width), in_hbm(tiles))


def boundary_forward_kernel(
    list_ref, group_ref, near_ref, start_ref, tiles_ref, sum_ref, table, total, store, sems, start_sem
):
    blocks, tile, width = sum_ref.shape
    group = near_ref.shape[0] // blocks
    begin, turns = group_ref[0, 1], group_ref[0, 4]
    start_copy = pltpu.make_async_copy(start_ref, total.at[pl.ds(0, blocks)], start_sem)
    start_copy.start()
    fetch_tiles(list_ref, begin, 0, turns, tiles_ref, store, sems)
    for b in range(blocks):
        table[b] = near_ref[b * group : (b + 1) * group, 0 : tile // group, :].reshape(tile, width)
    table[blocks] = jnp.zeros(table.shape[1:], BF16)
    start_copy.wait()
    tile_loop(list_ref, begin, 0, turns, tiles_ref, store, sems, forward_body(total, table, blocks))
    sum_ref[...] = total[:blocks]


def boundary_forward(lists, groups, arrived, start, tiles):
    blocks, tile, width = start.shape
    return pl.pallas_call(
        boundary_forward_kernel,
        name="boundary_forward",
        in_specs=[whole(SMEM)] * 2 + [whole(VMEM), whole(pltpu.HBM), whole(pltpu.HBM)],
        out_specs=whole(VMEM),
        out_shape=jax.ShapeDtypeStruct(start.shape, F32),
        scratch_shapes=[VMEM((blocks + 1, tile, width), BF16), VMEM((blocks + 1, tile, width), F32)]
        + store_scratch(tiles, blocks)
        + [pltpu.SemaphoreType.DMA],
        compiler_params=params(40),
        cost_estimate=pl.CostEstimate(flops=10**9, bytes_accessed=40 << 20, transcendentals=0),
    )(lists, groups, arrived, in_hbm(start), in_hbm(tiles))


def middle_kernel(
    list_ref, group_ref, near_ref, far_ref, hot_ref, start_ref, weight_ref, bias_ref, cot_ref, tiles_ref,
    act_out, back_out, grads_ref, act_ref, table, total, swapped, spread, parcel, store, sems, out_sems,
):
    blocks, tile, width = act_ref.shape
    group = near_ref.shape[0] // blocks
    rows = tile // group
    weight = weight_ref[...]
    near_turns, hub_turns = group_ref[0, 4], group_ref[0, 5]
    fetch_tiles(list_ref, group_ref[0, 2], 0, hub_turns, tiles_ref, store, sems)
    fetch_tiles(list_ref, group_ref[0, 1] - hub_turns, hub_turns, hub_turns + near_turns, tiles_ref, store, sems)
    total[:blocks] = start_ref[...]

    @pl.loop(0, blocks // 4)
    def _(turn):
        for i in range(4):
            b = turn * 4 + i
            near = near_ref[pl.ds(b * group, group), rows : 2 * rows, :].reshape(tile, width)
            far = far_ref[pl.ds(b * group, group), rows : 2 * rows, :].reshape(tile, width)
            picked = jnp.dot(hot_ref[b], jnp.concatenate([near, far], axis=0), preferred_element_type=F32)
            table[b] = picked.astype(BF16)

    table[blocks] = jnp.zeros(table.shape[1:], BF16)
    tile_loop(
        list_ref, group_ref[0, 2], 0, hub_turns, tiles_ref, store, sems, forward_body(total, table, 2 * blocks)
    )

    @pl.loop(0, blocks // 2)
    def _(turn):
        for i in range(2):
            b = turn * 2 + i
            preact = jnp.dot(total[b].astype(BF16), weight, preferred_element_type=F32) + bias_ref[...]
            sigmoid = 0.5 * jnp.tanh(0.5 * preact) + 0.5
            act_ref[b] = (preact * sigmoid).astype(BF16)
            slope = sigmoid * (1.0 + preact * (1.0 - sigmoid))
            upstream = (cot_ref[b].astype(F32) * slope).astype(BF16)
            swapped[b] = lax.dot_general(weight, upstream, NT, preferred_element_type=F32).astype(BF16)

    results = (
        pltpu.make_async_copy(act_ref, act_out, out_sems.at[blocks // 2]),
        pltpu.make_async_copy(swapped.at[pl.ds(0, blocks)], back_out, out_sems.at[blocks // 2 + 1]),
    )
    for result in results:
        result.start()
    spread[...] = jnp.zeros_like(spread)
    add = backward_body(spread, swapped, blocks)
    tile_loop(list_ref, group_ref[0, 2], 0, hub_turns, tiles_ref, store, None, add)
    tile_loop(
        list_ref, group_ref[0, 1] - hub_turns, hub_turns, hub_turns + near_turns, tiles_ref, store, sems, add
    )

    chunk = 2 * group

    def send(turn):
        return pltpu.make_async_copy(
            parcel.at[pl.ds(turn * chunk, chunk)], grads_ref.at[pl.ds(turn * chunk, chunk)], out_sems.at[turn]
        )

    @pl.loop(0, blocks // 2)
    def _(turn):
        for i in range(2):
            b = turn * 2 + i
            for part in range(2):
                out = jnp.transpose(spread[part * blocks + b].astype(BF16))
                parcel[pl.ds(b * group, group), part * rows : (part + 1) * rows, :] = out.reshape(
                    group, rows, width
                )
        send(turn).start()

    @pl.loop(0, blocks // 2)
    def _(turn):
        send(turn).wait()

    for result in results:
        result.wait()


def middle(lists, groups, arrived, other, hot, start, weight, bias, cotangent, tiles):
    blocks, tile, width = start.shape
    parties = arrived.shape[0]
    rows = blocks * tile // parties
    return pl.pallas_call(
        middle_kernel,
        name="middle",
        in_specs=[whole(SMEM)] * 2
        + [whole(VMEM)] * 7
        + [whole(pltpu.HBM)],
        out_specs=[whole(pltpu.HBM)] * 3,
        out_shape=[
            pltpu.HBM((blocks, tile, width), BF16),
            pltpu.HBM((blocks, width, tile), BF16),
            pltpu.HBM((parties, 2 * rows, width), BF16),
        ],
        scratch_shapes=[
            VMEM((blocks, tile, width), BF16),
            VMEM((blocks + 1, tile, width), BF16),
            VMEM((blocks + 1, tile, width), F32),
            VMEM((blocks + 1, width, tile), BF16),
            VMEM((2 * blocks + 1, width, tile), F32),
            VMEM((parties, 2 * rows, width), BF16),
        ]
        + store_scratch(tiles, blocks)
        + [pltpu.SemaphoreType.DMA((blocks // 2 + 2,))],
        compiler_params=params(42),
        cost_estimate=pl.CostEstimate(flops=4 * 10**9, bytes_accessed=60 << 20, transcendentals=10**6),
    )(
        lists, groups, arrived, other, hot, start, weight, bias, cotangent.reshape(blocks, tile, width), in_hbm(tiles)
    )


def own_backward_kernel(
    list_ref, group_ref, back_ref, names_ref, tiles_ref, own_ref, hot_ref, swapped, spread, store, sems, back_sem
):
    blocks = back_ref.shape[0]
    begin, turns = group_ref[0, 0], group_ref[0, 3]
    back_copy = pltpu.make_async_copy(back_ref, swapped.at[pl.ds(0, blocks)], back_sem)
    back_copy.start()
    fetch_tiles(list_ref, begin, 0, turns, tiles_ref, store, sems)
    spread[...] = jnp.zeros_like(spread)
    back_copy.wait()
    tile_loop(list_ref, begin, 0, turns, tiles_ref, store, sems, backward_body(spread, swapped, 0))

    @pl.loop(0, blocks // 2)
    def _(turn):
        for i in range(2):
            own_ref[turn * 2 + i] = jnp.transpose(spread[turn * 2 + i])

    parties, total, width = names_ref.shape
    group = parties // blocks
    rows = width // group
    names = names_ref[:, total - 8, :].astype(F32)
    party = lax.broadcasted_iota(I32, names.shape, 0)
    lane = lax.broadcasted_iota(I32, names.shape, 1)
    names = jnp.where(lane // rows == party % group, names, 0.0).astype(BF16)
    block = lax.broadcasted_iota(I32, (blocks, parties), 0)
    gather = jnp.where(lax.broadcasted_iota(I32, (blocks, parties), 1) // group == block, 1.0, 0.0)
    lines = jnp.dot(gather.astype(BF16), names, preferred_element_type=F32)
    hub = lax.broadcasted_iota(I32, hot_ref.shape[1:], 0).astype(F32)
    for b in range(blocks):
        hot_ref[b] = jnp.where(hub == lines[b : b + 1, :], 1.0, 0.0).astype(BF16)


def own_backward(lists, groups, back, arrived, tiles, hubs):
    blocks, width, tile = back.shape
    return pl.pallas_call(
        own_backward_kernel,
        name="own_backward",
        in_specs=[whole(SMEM)] * 2 + [whole(pltpu.HBM), whole(VMEM), whole(pltpu.HBM)],
        out_specs=[whole(VMEM)] * 2,
        out_shape=[
            jax.ShapeDtypeStruct((blocks, tile, width), F32),
            jax.ShapeDtypeStruct((blocks, hubs, width), BF16),
        ],
        scratch_shapes=[VMEM((blocks + 1, width, tile), BF16), VMEM((blocks + 1, width, tile), F32)]
        + store_scratch(tiles, blocks)
        + [pltpu.SemaphoreType.DMA],
        compiler_params=params(50),
        cost_estimate=pl.CostEstimate(flops=10**9, bytes_accessed=40 << 20, transcendentals=0),
    )(lists, groups, in_hbm(back), arrived, in_hbm(tiles))


def returned_kernel(send_ref, own_ref, back_ref, hot_ref, sal_out, hub_ref, stage, hot, first, chains, sems):
    rows, parties = send_ref.shape
    blocks, _, width = hot_ref.shape
    group = parties // blocks
    own_copy = pltpu.make_async_copy(own_ref, first, sems.at[0])
    hot_copy = pltpu.make_async_copy(hot_ref, hot, sems.at[1])
    own_copy.start()
    hot_copy.start()
    for chain in chains:
        chain[...] = jnp.zeros_like(chain)

    @pl.loop(0, parties // 4)
    def _(turn):
        for i in range(4):
            stage[turn * 4 + i] = back_ref[turn * 4 + i, 0:rows, :].astype(F32)

    own_copy.wait()
    sums = (first,) + tuple(chains)

    @pl.loop(0, rows)
    def _(j):
        for q in range(parties):
            chain = sums[q % len(sums)]
            row = send_ref[j, q]
            chain[pl.ds(row, 1), :] += stage[q, pl.ds(j, 1), :]

    turns = sems.shape[0] - 2
    size = first.shape[0] // turns

    def result(turn):
        part = pl.ds(turn * size, size)
        return pltpu.make_async_copy(first.at[part], sal_out.at[part], sems.at[turn + 2])

    @pl.loop(0, turns)
    def _(turn):
        part = pl.ds(turn * size, size)
        total = first[part, :]
        for chain in chains:
            total = total + chain[part, :]
        first[part, :] = total
        result(turn).start()

    hot_copy.wait()
    total = jnp.zeros(hub_ref.shape, F32)
    for b in range(0, blocks, 2):
        grads = back_ref[b * group : (b + 2) * group, rows:, :].reshape(2 * group * rows, width)
        pair = jnp.concatenate([hot[b], hot[b + 1]], axis=1)
        total += jnp.dot(pair, grads, preferred_element_type=F32)
    hub_ref[...] = total

    @pl.loop(0, turns)
    def _(turn):
        result(turn).wait()


def returned_rows(send, own, returned, hot):
    rows, parties = send.shape
    own_rows, width = own.shape
    return pl.pallas_call(
        returned_kernel,
        name="returned_rows",
        in_specs=[whole(SMEM), whole(pltpu.HBM), whole(VMEM), whole(pltpu.HBM)],
        out_specs=[whole(pltpu.HBM), whole(VMEM)],
        out_shape=[
            pltpu.HBM((own_rows, width), F32),
            jax.ShapeDtypeStruct((hot.shape[1], width), F32),
        ],
        scratch_shapes=[
            VMEM((parties, rows, width), F32),
            VMEM(hot.shape, BF16),
            VMEM((own_rows, width), F32),
            [VMEM((own_rows, width), F32)] * (CHAINS - 1),
            pltpu.SemaphoreType.DMA((2 + 16,)),
        ],
        compiler_params=params(32),
        cost_estimate=pl.CostEstimate(flops=10**8, bytes_accessed=40 << 20, transcendentals=0),
    )(send, in_hbm(own), returned, in_hbm(hot))


def body(
    features, hubs, weight, bias, cotangent, tiles, tile_blocks, tile_count, halo_send, replica_rows
):
    own_rows, width = features.shape
    tile = tiles.shape[1]
    blocks = own_rows // tile
    send = halo_send[0].T
    wanted = replica_rows[0].T
    parties = send.shape[1]
    side = (lax.axis_index("dom") % 2).astype(I32).reshape(1)

    pairs = [(i, i ^ 1) for i in range(parties)]

    outgoing = outgoing_rows(send, features, hubs, wanted)
    arrived = lax.all_to_all(outgoing, "dom", split_axis=0, concat_axis=0, tiled=True)
    lists, groups, hot = plan(tile_count, side, tile_blocks.T, wanted, blocks, tile)
    start = own_forward(lists, groups, features, tiles)
    other = lax.ppermute(arrived, "dom", pairs)
    start = boundary_forward(lists, groups, arrived, start, tiles)
    act, back, grads = middle(lists, groups, arrived, other, hot, start, weight, bias.reshape(1, -1), cotangent, tiles)
    returned = lax.all_to_all(grads, "dom", split_axis=0, concat_axis=0, tiled=True)
    own, hub_hot = own_backward(lists, groups, back, arrived, tiles, hubs.shape[0])
    saliency, hub_saliency = returned_rows(send, own.reshape(own_rows, width), returned, hub_hot)
    return act.reshape(own_rows, width), saliency, hub_saliency


def solution(mesh):
    placed = (
        P("dom", None),
        P("dom", None),
        P(),
        P(),
        P("dom", None),
        P("dom", None, None),
        P("dom", None),
        P("dom"),
        P("dom", None, None),
        P("dom", None, None),
    )
    return jax.shard_map(
        body,
        mesh=mesh,
        in_specs=placed,
        out_specs=(P("dom", None), P("dom", None), P("dom", None)),
        check_vma=False,
    )
```

```python
import functools

import jax
import jax.numpy as jnp
from jax import lax
from jax.experimental import pallas as pl
from jax.experimental.pallas import tpu as pltpu
from jax.sharding import PartitionSpec as P


VMEM = pltpu.VMEM
SMEM = pltpu.SMEM
F32 = jnp.float32
BF16 = jnp.bfloat16
I32 = jnp.int32
PAIRS = 8
CHAINS = 8
ACT = 8
TURNS = 16
NT = (((1,), (1,)), ((), ()))


def whole(space):
    return pl.BlockSpec(memory_space=space)


def params(mib):
    return pltpu.CompilerParams(vmem_limit_bytes=mib << 20)


def in_hbm(array):
    return pltpu.with_memory_space_constraint(array, pltpu.HBM)


def outgoing_kernel(send_ref, feat_ref, hub_ref, wanted_ref, out_ref, wide, stage, names, parcel, sems):
    rows, parties = send_ref.shape
    width = feat_ref.shape[1]
    half = hub_ref.shape[0] // 2
    wide[...] = feat_ref[...].astype(F32)
    tall = jnp.concatenate([wanted_ref[...].astype(F32)] * (width // rows), axis=0)
    names[...] = jnp.transpose(tall)

    @pl.loop(0, rows)
    def _(j):
        for q in range(parties):
            stage[q, pl.ds(j, 1), :] = wide[pl.ds(send_ref[j, q], 1), :]

    halves = (hub_ref[:half, :], hub_ref[half:, :])
    turns = sems.shape[0]
    chunk = parties // turns

    def send(turn):
        part = pl.ds(turn * chunk, chunk)
        return pltpu.make_async_copy(parcel.at[part], out_ref.at[part], sems.at[turn])

    @pl.loop(0, turns)
    def _(turn):
        for i in range(chunk):
            q = turn * chunk + i
            parcel[q, 0:rows, :] = stage[q].astype(BF16)
            parcel[q, rows : rows + half, :] = halves[i % 2]
            line = names[pl.ds(q, 1), :]
            parcel[q, rows + half :, :] = jnp.broadcast_to(line, (8, width)).astype(BF16)
        send(turn).start()

    @pl.loop(0, turns)
    def _(turn):
        send(turn).wait()


def outgoing_rows(send, features, hubs, wanted):
    rows, parties = send.shape
    width = features.shape[1]
    total = rows + hubs.shape[0] // 2 + 8
    return pl.pallas_call(
        outgoing_kernel,
        name="outgoing_rows",
        in_specs=[whole(SMEM)] + [whole(VMEM)] * 3,
        out_specs=whole(pltpu.HBM),
        out_shape=pltpu.HBM((parties, total, width), BF16),
        scratch_shapes=[
            VMEM(features.shape, F32),
            VMEM((parties, rows, width), F32),
            VMEM((parties, width), F32),
            VMEM((parties, total, width), BF16),
            pltpu.SemaphoreType.DMA((16,)),
        ],
        compiler_params=params(60),
        cost_estimate=pl.CostEstimate(flops=0, bytes_accessed=30 << 20, transcendentals=0),
    )(send, features, hubs, wanted)


def plan_kernel(blocks, count_ref, side_ref, places_ref, wanted_ref, list_ref, group_ref, hot_ref):
    slots = places_ref.shape[1]
    length = list_ref.shape[1]
    lanes = 128
    count = count_ref[0]
    row = places_ref[0:1, :]
    column = places_ref[1:2, :]
    slot = lax.broadcasted_iota(I32, (1, slots), 1)
    kind = jnp.where(column < blocks, 0, jnp.where(column < 2 * blocks, 1, 2))
    key = jnp.where(slot < count, kind * blocks + row, lanes - 1).astype(F32)
    entry = (slot | (row << 10) | (column << 16)).astype(F32)
    lines = jnp.concatenate([key, entry] + [jnp.zeros_like(key)] * 6, axis=0)
    tall = jnp.transpose(lines)
    key_tall, entry_tall = tall[:, 0:1], tall[:, 1:2]
    lane = lax.broadcasted_iota(I32, (1, lanes), 1)
    member = key_tall == lane.astype(F32)
    counts = jnp.sum(jnp.where(member, 1.0, 0.0), axis=0, keepdims=True)
    halves = jnp.where(lane < 3 * blocks, (counts.astype(I32) + 1) // 2, 0)
    before = jnp.where(
        lax.broadcasted_iota(I32, (lanes, lanes), 0) < lax.broadcasted_iota(I32, (lanes, lanes), 1), 1.0, 0.0
    ).astype(BF16)
    prefix = jnp.dot(
        jnp.broadcast_to(halves.astype(F32), (16, lanes)).astype(BF16), before, preferred_element_type=F32
    )[0:1, :].astype(I32)
    bucket = lane // blocks
    offset = prefix
    groups = jnp.zeros_like(lane)
    begun = jnp.zeros((1, 1), I32)
    passed = jnp.zeros((1, 1), I32)
    for k in range(3):
        pairs = jnp.sum(jnp.where(bucket == k, halves, 0), axis=1, keepdims=True)
        turns = (pairs + PAIRS - 1) // PAIRS
        offset = jnp.where(bucket == k, prefix + (begun * PAIRS - passed), offset)
        groups = jnp.where(lane == k, begun, groups)
        groups = jnp.where(lane == 3 + k, turns, groups)
        begun = begun + turns
        passed = passed + pairs
    group_ref[...] = groups
    first = jnp.sum(jnp.where(member, offset.astype(F32), 0.0), axis=1, keepdims=True)
    earlier = lax.broadcasted_iota(I32, (slots, slots), 1) < lax.broadcasted_iota(I32, (slots, slots), 0)
    index = jnp.sum(jnp.where((key_tall == key) & earlier, 1.0, 0.0), axis=1, keepdims=True)
    place = jnp.where(key_tall < 3 * blocks, 2.0 * first + index, -1.0)
    spare = float((blocks << 10) | (3 * blocks << 16))
    target = lax.broadcasted_iota(I32, (1, length), 1).astype(F32)
    placed = jnp.sum(jnp.where(place == target, entry_tall - spare, 0.0), axis=0, keepdims=True)
    list_ref[...] = (placed + spare).astype(I32)

    rows, parties = wanted_ref.shape
    group = hot_ref.shape[1] // rows
    half = hot_ref.shape[2] // 2 // group
    wanted = wanted_ref[...]
    member_of = lax.broadcasted_iota(I32, (rows, parties), 1) % group
    far = ((wanted >= half).astype(I32) != side_ref[0]).astype(I32)
    spot = jnp.where(wanted >= half, wanted - half, wanted) + member_of * half + far * (group * half)
    lane = lax.broadcasted_iota(I32, (rows, 2 * group * half), 1)
    for p in range(parties):
        hot = jnp.where(spot[:, p : p + 1] == lane, 1.0, 0.0)
        hot_ref[p // group, (p % group) * rows : (p % group + 1) * rows, :] = hot.astype(BF16)


def plan(count, side, places, wanted, blocks, tile):
    slots = places.shape[1]
    length = list_length(slots, blocks)
    return pl.pallas_call(
        functools.partial(plan_kernel, blocks),
        name="plan",
        in_specs=[whole(SMEM), whole(SMEM), whole(VMEM), whole(VMEM)],
        out_specs=[whole(VMEM)] * 3,
        out_shape=[
            jax.ShapeDtypeStruct((1, length), I32),
            jax.ShapeDtypeStruct((1, 128), I32),
            jax.ShapeDtypeStruct((blocks, tile, 2 * tile), BF16),
        ],
        compiler_params=params(60),
        cost_estimate=pl.CostEstimate(flops=10**7, bytes_accessed=8 << 20, transcendentals=0),
    )(count, side, places, wanted)


def unpack(entry):
    return entry & 1023, (entry >> 10) & 63, entry >> 16


def fetch_tiles(list_ref, begin, first, last, tiles_ref, store, sems):
    @pl.loop(first, last)
    def _(turn):
        for u in range(2 * PAIRS):
            tile, _, _ = unpack(list_ref[0, (begin + turn) * 2 * PAIRS + u])
            pltpu.make_async_copy(tiles_ref.at[tile], store.at[turn, u], sems.at[turn]).start()


def tile_loop(list_ref, begin, first, last, tiles_ref, store, sems, body):
    @pl.loop(first, last)
    def _(turn):
        if sems is not None:
            pltpu.make_async_copy(
                tiles_ref.at[pl.ds(0, 2 * PAIRS)], store.at[turn], sems.at[turn]
            ).wait()
        for u in range(PAIRS):
            place = (begin + turn) * 2 * PAIRS + 2 * u
            _, row, left = unpack(list_ref[0, place])
            _, _, right = unpack(list_ref[0, place + 1])
            body(store[turn, 2 * u], store[turn, 2 * u + 1], row, left, right)


def list_length(slots, blocks):
    return -(-(slots + 3 * blocks + 6 * PAIRS) // 128) * 128


def store_scratch(tiles, blocks):
    groups = (tiles.shape[0] + 3 * blocks) // (2 * PAIRS) + 4
    return [
        VMEM((groups, 2 * PAIRS) + tiles.shape[1:], BF16),
        pltpu.SemaphoreType.DMA((groups,)),
    ]


def forward_body(total, table, base):
    spare = table.shape[0] - 1

    def body(first, second, row, left, right):
        values = jnp.concatenate([first, second], axis=1)
        left = jnp.minimum(left - base, spare)
        right = jnp.minimum(right - base, spare)
        rows = jnp.concatenate([table[left], table[right]], axis=0)
        total[row] += jnp.dot(values, rows, preferred_element_type=F32)

    return body


def backward_body(spread, swapped, base):
    spare = spread.shape[0] - 1

    def body(first, second, row, left, right):
        tile = first.shape[1]
        values = jnp.concatenate([first, second], axis=1)
        product = jnp.dot(swapped[row], values, preferred_element_type=F32)
        spread[jnp.minimum(left - base, spare)] += product[:, :tile]
        spread[jnp.minimum(right - base, spare)] += product[:, tile:]

    return body


def own_forward_kernel(list_ref, group_ref, feat_ref, tiles_ref, sum_ref, table, total, store, sems):
    blocks = feat_ref.shape[0]
    begin, turns = group_ref[0, 0], group_ref[0, 3]
    fetch_tiles(list_ref, begin, 0, turns, tiles_ref, store, sems)
    total[...] = jnp.zeros_like(total)
    table[:blocks] = feat_ref[...]
    table[blocks] = jnp.zeros(table.shape[1:], BF16)
    tile_loop(list_ref, begin, 0, turns, tiles_ref, store, sems, forward_body(total, table, 0))
    sum_ref[...] = total[:blocks]


def own_forward(lists, groups, features, tiles):
    tile = tiles.shape[1]
    blocks = features.shape[0] // tile
    width = features.shape[1]
    return pl.pallas_call(
        own_forward_kernel,
        name="own_forward",
        in_specs=[whole(SMEM), whole(SMEM), whole(VMEM), whole(pltpu.HBM)],
        out_specs=whole(VMEM),
        out_shape=jax.ShapeDtypeStruct((blocks, tile, width), F32),
        scratch_shapes=[VMEM((blocks + 1, tile, width), BF16), VMEM((blocks + 1, tile, width), F32)]
        + store_scratch(tiles, blocks),
        compiler_params=params(50),
        cost_estimate=pl.CostEstimate(flops=10**9, bytes_accessed=40 << 20, transcendentals=0),
    )(lists, groups, features.reshape(blocks, tile, width), in_hbm(tiles))


def boundary_forward_kernel(
    list_ref, group_ref, near_ref, tiles_ref, sum_ref, table, total, store, sems
):
    blocks, tile, width = sum_ref.shape
    group = near_ref.shape[0] // blocks
    begin, turns = group_ref[0, 1], group_ref[0, 4]
    fetch_tiles(list_ref, begin, 0, turns, tiles_ref, store, sems)
    total[...] = jnp.zeros_like(total)
    for b in range(blocks):
        table[b] = near_ref[b * group : (b + 1) * group, 0 : tile // group, :].reshape(tile, width)
    table[blocks] = jnp.zeros(table.shape[1:], BF16)
    tile_loop(list_ref, begin, 0, turns, tiles_ref, store, sems, forward_body(total, table, blocks))
    sum_ref[...] = total[:blocks]


def boundary_forward(lists, groups, arrived, blocks, tiles):
    tile, width = tiles.shape[1], arrived.shape[2]
    return pl.pallas_call(
        boundary_forward_kernel,
        name="boundary_forward",
        in_specs=[whole(SMEM)] * 2 + [whole(VMEM), whole(pltpu.HBM)],
        out_specs=whole(VMEM),
        out_shape=jax.ShapeDtypeStruct((blocks, tile, width), F32),
        scratch_shapes=[VMEM((blocks + 1, tile, width), BF16), VMEM((blocks + 1, tile, width), F32)]
        + store_scratch(tiles, blocks),
        compiler_params=params(40),
        cost_estimate=pl.CostEstimate(flops=10**9, bytes_accessed=40 << 20, transcendentals=0),
    )(lists, groups, arrived, in_hbm(tiles))


def middle_kernel(
    list_ref, group_ref, near_ref, far_ref, hot_ref, start_ref, part_ref, weight_ref, bias_ref, cot_ref, tiles_ref,
    act_out, back_out, grads_ref, act_ref, table, total, swapped, spread, parcel, store, sems, out_sems,
):
    blocks, tile, width = act_ref.shape
    group = near_ref.shape[0] // blocks
    rows = tile // group
    weight = weight_ref[...]
    start_copy = pltpu.make_async_copy(start_ref, total.at[pl.ds(0, blocks)], out_sems.at[blocks // 2])
    start_copy.start()
    near_turns, hub_turns = group_ref[0, 4], group_ref[0, 5]
    fetch_tiles(list_ref, group_ref[0, 2], 0, hub_turns, tiles_ref, store, sems)
    fetch_tiles(list_ref, group_ref[0, 1] - hub_turns, hub_turns, hub_turns + near_turns, tiles_ref, store, sems)

    @pl.loop(0, blocks // 4)
    def _(turn):
        for i in range(4):
            b = turn * 4 + i
            near = near_ref[pl.ds(b * group, group), rows : 2 * rows, :].reshape(tile, width)
            far = far_ref[pl.ds(b * group, group), rows : 2 * rows, :].reshape(tile, width)
            picked = jnp.dot(hot_ref[b], jnp.concatenate([near, far], axis=0), preferred_element_type=F32)
            table[b] = picked.astype(BF16)

    start_copy.wait()
    total[:blocks] += part_ref[...]
    table[blocks] = jnp.zeros(table.shape[1:], BF16)
    tile_loop(
        list_ref, group_ref[0, 2], 0, hub_turns, tiles_ref, store, sems, forward_body(total, table, 2 * blocks)
    )

    @pl.loop(0, blocks // ACT)
    def _(turn):
        for i in range(ACT):
            b = turn * ACT + i
            preact = jnp.dot(total[b].astype(BF16), weight, preferred_element_type=F32) + bias_ref[...]
            sigmoid = 0.5 * jnp.tanh(0.5 * preact) + 0.5
            act_ref[b] = (preact * sigmoid).astype(BF16)
            slope = sigmoid * (1.0 + preact * (1.0 - sigmoid))
            upstream = (cot_ref[b].astype(F32) * slope).astype(BF16)
            swapped[b] = lax.dot_general(weight, upstream, NT, preferred_element_type=F32).astype(BF16)

    results = (
        pltpu.make_async_copy(act_ref, act_out, out_sems.at[blocks // 2]),
        pltpu.make_async_copy(swapped.at[pl.ds(0, blocks)], back_out, out_sems.at[blocks // 2 + 1]),
    )
    for result in results:
        result.start()
    spread[...] = jnp.zeros_like(spread)
    add = backward_body(spread, swapped, blocks)
    tile_loop(list_ref, group_ref[0, 2], 0, hub_turns, tiles_ref, store, None, add)
    tile_loop(
        list_ref, group_ref[0, 1] - hub_turns, hub_turns, hub_turns + near_turns, tiles_ref, store, sems, add
    )

    chunk = 2 * group

    def send(turn):
        return pltpu.make_async_copy(
            parcel.at[pl.ds(turn * chunk, chunk)], grads_ref.at[pl.ds(turn * chunk, chunk)], out_sems.at[turn]
        )

    @pl.loop(0, blocks // 2)
    def _(turn):
        for i in range(2):
            b = turn * 2 + i
            for part in range(2):
                out = jnp.transpose(spread[part * blocks + b].astype(BF16))
                parcel[pl.ds(b * group, group), part * rows : (part + 1) * rows, :] = out.reshape(
                    group, rows, width
                )
        send(turn).start()

    @pl.loop(0, blocks // 2)
    def _(turn):
        send(turn).wait()

    for result in results:
        result.wait()


def middle(lists, groups, arrived, other, hot, start, near, weight, bias, cotangent, tiles):
    blocks, tile, width = start.shape
    parties = arrived.shape[0]
    rows = blocks * tile // parties
    return pl.pallas_call(
        middle_kernel,
        name="middle",
        in_specs=[whole(SMEM)] * 2
        + [whole(VMEM)] * 3
        + [whole(pltpu.HBM)]
        + [whole(VMEM)] * 4
        + [whole(pltpu.HBM)],
        out_specs=[whole(pltpu.HBM)] * 3,
        out_shape=[
            pltpu.HBM((blocks, tile, width), BF16),
            pltpu.HBM((blocks, width, tile), BF16),
            pltpu.HBM((parties, 2 * rows, width), BF16),
        ],
        scratch_shapes=[
            VMEM((blocks, tile, width), BF16),
            VMEM((blocks + 1, tile, width), BF16),
            VMEM((blocks + 1, tile, width), F32),
            VMEM((blocks + 1, width, tile), BF16),
            VMEM((2 * blocks + 1, width, tile), F32),
            VMEM((parties, 2 * rows, width), BF16),
        ]
        + store_scratch(tiles, blocks)
        + [pltpu.SemaphoreType.DMA((blocks // 2 + 2,))],
        compiler_params=params(42),
        cost_estimate=pl.CostEstimate(flops=4 * 10**9, bytes_accessed=60 << 20, transcendentals=10**6),
    )(
        lists, groups, arrived, other, hot, in_hbm(start), near, weight, bias, cotangent.reshape(blocks, tile, width), in_hbm(tiles)
    )


def own_backward_kernel(
    list_ref, group_ref, back_ref, names_ref, tiles_ref, own_ref, hot_ref, swapped, spread, store, sems, back_sem
):
    blocks = back_ref.shape[0]
    begin, turns = group_ref[0, 0], group_ref[0, 3]
    back_copy = pltpu.make_async_copy(back_ref, swapped.at[pl.ds(0, blocks)], back_sem)
    back_copy.start()
    fetch_tiles(list_ref, begin, 0, turns, tiles_ref, store, sems)
    spread[...] = jnp.zeros_like(spread)
    back_copy.wait()
    tile_loop(list_ref, begin, 0, turns, tiles_ref, store, sems, backward_body(spread, swapped, 0))

    @pl.loop(0, blocks // 2)
    def _(turn):
        for i in range(2):
            own_ref[turn * 2 + i] = jnp.transpose(spread[turn * 2 + i])

    parties, total, width = names_ref.shape
    group = parties // blocks
    rows = width // group
    names = names_ref[:, total - 8, :].astype(F32)
    party = lax.broadcasted_iota(I32, names.shape, 0)
    lane = lax.broadcasted_iota(I32, names.shape, 1)
    names = jnp.where(lane // rows == party % group, names, 0.0).astype(BF16)
    block = lax.broadcasted_iota(I32, (blocks, parties), 0)
    gather = jnp.where(lax.broadcasted_iota(I32, (blocks, parties), 1) // group == block, 1.0, 0.0)
    lines = jnp.dot(gather.astype(BF16), names, preferred_element_type=F32)
    hub = lax.broadcasted_iota(I32, hot_ref.shape[1:], 0).astype(F32)
    for b in range(blocks):
        hot_ref[b] = jnp.where(hub == lines[b : b + 1, :], 1.0, 0.0).astype(BF16)


def own_backward(lists, groups, back, arrived, tiles, hubs):
    blocks, width, tile = back.shape
    return pl.pallas_call(
        own_backward_kernel,
        name="own_backward",
        in_specs=[whole(SMEM)] * 2 + [whole(pltpu.HBM), whole(VMEM), whole(pltpu.HBM)],
        out_specs=[whole(VMEM)] * 2,
        out_shape=[
            jax.ShapeDtypeStruct((blocks, tile, width), F32),
            jax.ShapeDtypeStruct((blocks, hubs, width), BF16),
        ],
        scratch_shapes=[VMEM((blocks + 1, width, tile), BF16), VMEM((blocks + 1, width, tile), F32)]
        + store_scratch(tiles, blocks)
        + [pltpu.SemaphoreType.DMA],
        compiler_params=params(50),
        cost_estimate=pl.CostEstimate(flops=10**9, bytes_accessed=40 << 20, transcendentals=0),
    )(lists, groups, in_hbm(back), arrived, in_hbm(tiles))


def returned_kernel(send_ref, own_ref, back_ref, hot_ref, sal_out, hub_ref, stage, hot, first, chains, sems):
    rows, parties = send_ref.shape
    blocks, _, width = hot_ref.shape
    group = parties // blocks
    own_copy = pltpu.make_async_copy(own_ref, first, sems.at[0])
    hot_copy = pltpu.make_async_copy(hot_ref, hot, sems.at[1])
    own_copy.start()
    hot_copy.start()
    for chain in chains:
        chain[...] = jnp.zeros_like(chain)

    @pl.loop(0, parties // 4)
    def _(turn):
        for i in range(4):
            stage[turn * 4 + i] = back_ref[turn * 4 + i, 0:rows, :].astype(F32)

    own_copy.wait()
    sums = (first,) + tuple(chains)

    @pl.loop(0, rows)
    def _(j):
        for q in range(parties):
            chain = sums[q % len(sums)]
            row = send_ref[j, q]
            chain[pl.ds(row, 1), :] += stage[q, pl.ds(j, 1), :]

    turns = sems.shape[0] - 2
    size = first.shape[0] // turns

    def result(turn):
        part = pl.ds(turn * size, size)
        return pltpu.make_async_copy(first.at[part], sal_out.at[part], sems.at[turn + 2])

    @pl.loop(0, turns)
    def _(turn):
        part = pl.ds(turn * size, size)
        total = first[part, :]
        for chain in chains:
            total = total + chain[part, :]
        first[part, :] = total
        result(turn).start()

    hot_copy.wait()
    total = jnp.zeros(hub_ref.shape, F32)
    for b in range(0, blocks, 2):
        grads = back_ref[b * group : (b + 2) * group, rows:, :].reshape(2 * group * rows, width)
        pair = jnp.concatenate([hot[b], hot[b + 1]], axis=1)
        total += jnp.dot(pair, grads, preferred_element_type=F32)
    hub_ref[...] = total

    @pl.loop(0, turns)
    def _(turn):
        result(turn).wait()


def returned_rows(send, own, returned, hot):
    rows, parties = send.shape
    own_rows, width = own.shape
    return pl.pallas_call(
        returned_kernel,
        name="returned_rows",
        in_specs=[whole(SMEM), whole(pltpu.HBM), whole(VMEM), whole(pltpu.HBM)],
        out_specs=[whole(pltpu.HBM), whole(VMEM)],
        out_shape=[
            pltpu.HBM((own_rows, width), F32),
            jax.ShapeDtypeStruct((hot.shape[1], width), F32),
        ],
        scratch_shapes=[
            VMEM((parties, rows, width), F32),
            VMEM(hot.shape, BF16),
            VMEM((own_rows, width), F32),
            [VMEM((own_rows, width), F32)] * (CHAINS - 1),
            pltpu.SemaphoreType.DMA((2 + TURNS,)),
        ],
        compiler_params=params(32),
        cost_estimate=pl.CostEstimate(flops=10**8, bytes_accessed=40 << 20, transcendentals=0),
    )(send, in_hbm(own), returned, in_hbm(hot))


def body(
    features, hubs, weight, bias, cotangent, tiles, tile_blocks, tile_count, halo_send, replica_rows
):
    own_rows, width = features.shape
    tile = tiles.shape[1]
    blocks = own_rows // tile
    send = halo_send[0].T
    wanted = replica_rows[0].T
    parties = send.shape[1]
    side = (lax.axis_index("dom") % 2).astype(I32).reshape(1)

    pairs = [(i, i ^ 1) for i in range(parties)]

    outgoing = outgoing_rows(send, features, hubs, wanted)
    arrived = lax.all_to_all(outgoing, "dom", split_axis=0, concat_axis=0, tiled=True)
    lists, groups, hot = plan(tile_count, side, tile_blocks.T, wanted, blocks, tile)
    start = own_forward(lists, groups, features, tiles)
    other = lax.ppermute(arrived, "dom", pairs)
    near = boundary_forward(lists, groups, arrived, blocks, tiles)
    act, back, grads = middle(
        lists, groups, arrived, other, hot, start, near, weight, bias.reshape(1, -1), cotangent, tiles
    )
    returned = lax.all_to_all(grads, "dom", split_axis=0, concat_axis=0, tiled=True)
    own, hub_hot = own_backward(lists, groups, back, arrived, tiles, hubs.shape[0])
    saliency, hub_saliency = returned_rows(send, own.reshape(own_rows, width), returned, hub_hot)
    return act.reshape(own_rows, width), saliency, hub_saliency


def solution(mesh):
    placed = (
        P("dom", None),
        P("dom", None),
        P(),
        P(),
        P("dom", None),
        P("dom", None, None),
        P("dom", None),
        P("dom"),
        P("dom", None, None),
        P("dom", None, None),
    )
    return jax.shard_map(
        body,
        mesh=mesh,
        in_specs=placed,
        out_specs=(P("dom", None), P("dom", None), P("dom", None)),
        check_vma=False,
    )
```

```python
import functools

import jax
import jax.numpy as jnp
from jax import lax
from jax.experimental import pallas as pl
from jax.experimental.pallas import tpu as pltpu
from jax.sharding import PartitionSpec as P


VMEM = pltpu.VMEM
SMEM = pltpu.SMEM
F32 = jnp.float32
BF16 = jnp.bfloat16
I32 = jnp.int32
PAIRS = 8
CHAINS = 8
ACT = 16
TURNS = 16
NT = (((1,), (1,)), ((), ()))


def whole(space):
    return pl.BlockSpec(memory_space=space)


def params(mib):
    return pltpu.CompilerParams(vmem_limit_bytes=mib << 20)


def in_hbm(array):
    return pltpu.with_memory_space_constraint(array, pltpu.HBM)


def outgoing_kernel(send_ref, feat_ref, hub_ref, wanted_ref, out_ref, wide, stage, names, parcel, sems):
    rows, parties = send_ref.shape
    width = feat_ref.shape[1]
    half = hub_ref.shape[0] // 2
    wide[...] = feat_ref[...].astype(F32)
    tall = jnp.concatenate([wanted_ref[...].astype(F32)] * (width // rows), axis=0)
    names[...] = jnp.transpose(tall)

    @pl.loop(0, rows)
    def _(j):
        for q in range(parties):
            stage[q, pl.ds(j, 1), :] = wide[pl.ds(send_ref[j, q], 1), :]

    halves = (hub_ref[:half, :], hub_ref[half:, :])
    turns = sems.shape[0]
    chunk = parties // turns

    def send(turn):
        part = pl.ds(turn * chunk, chunk)
        return pltpu.make_async_copy(parcel.at[part], out_ref.at[part], sems.at[turn])

    @pl.loop(0, turns)
    def _(turn):
        for i in range(chunk):
            q = turn * chunk + i
            parcel[q, 0:rows, :] = stage[q].astype(BF16)
            parcel[q, rows : rows + half, :] = halves[i % 2]
            line = names[pl.ds(q, 1), :]
            parcel[q, rows + half :, :] = jnp.broadcast_to(line, (8, width)).astype(BF16)
        send(turn).start()

    @pl.loop(0, turns)
    def _(turn):
        send(turn).wait()


def outgoing_rows(send, features, hubs, wanted):
    rows, parties = send.shape
    width = features.shape[1]
    total = rows + hubs.shape[0] // 2 + 8
    return pl.pallas_call(
        outgoing_kernel,
        name="outgoing_rows",
        in_specs=[whole(SMEM)] + [whole(VMEM)] * 3,
        out_specs=whole(pltpu.HBM),
        out_shape=pltpu.HBM((parties, total, width), BF16),
        scratch_shapes=[
            VMEM(features.shape, F32),
            VMEM((parties, rows, width), F32),
            VMEM((parties, width), F32),
            VMEM((parties, total, width), BF16),
            pltpu.SemaphoreType.DMA((16,)),
        ],
        compiler_params=params(60),
        cost_estimate=pl.CostEstimate(flops=0, bytes_accessed=30 << 20, transcendentals=0),
    )(send, features, hubs, wanted)


def plan_kernel(blocks, count_ref, side_ref, places_ref, wanted_ref, list_ref, group_ref, hot_ref):
    slots = places_ref.shape[1]
    length = list_ref.shape[1]
    lanes = 128
    count = count_ref[0]
    row = places_ref[0:1, :]
    column = places_ref[1:2, :]
    slot = lax.broadcasted_iota(I32, (1, slots), 1)
    kind = jnp.where(column < blocks, 0, jnp.where(column < 2 * blocks, 1, 2))
    key = jnp.where(slot < count, kind * blocks + row, lanes - 1).astype(F32)
    entry = (slot | (row << 10) | (column << 16)).astype(F32)
    lines = jnp.concatenate([key, entry] + [jnp.zeros_like(key)] * 6, axis=0)
    tall = jnp.transpose(lines)
    key_tall, entry_tall = tall[:, 0:1], tall[:, 1:2]
    lane = lax.broadcasted_iota(I32, (1, lanes), 1)
    member = key_tall == lane.astype(F32)
    counts = jnp.sum(jnp.where(member, 1.0, 0.0), axis=0, keepdims=True)
    halves = jnp.where(lane < 3 * blocks, (counts.astype(I32) + 1) // 2, 0)
    before = jnp.where(
        lax.broadcasted_iota(I32, (lanes, lanes), 0) < lax.broadcasted_iota(I32, (lanes, lanes), 1), 1.0, 0.0
    ).astype(BF16)
    prefix = jnp.dot(
        jnp.broadcast_to(halves.astype(F32), (16, lanes)).astype(BF16), before, preferred_element_type=F32
    )[0:1, :].astype(I32)
    bucket = lane // blocks
    offset = prefix
    groups = jnp.zeros_like(lane)
    begun = jnp.zeros((1, 1), I32)
    passed = jnp.zeros((1, 1), I32)
    for k in range(3):
        pairs = jnp.sum(jnp.where(bucket == k, halves, 0), axis=1, keepdims=True)
        turns = (pairs + PAIRS - 1) // PAIRS
        offset = jnp.where(bucket == k, prefix + (begun * PAIRS - passed), offset)
        groups = jnp.where(lane == k, begun, groups)
        groups = jnp.where(lane == 3 + k, turns, groups)
        begun = begun + turns
        passed = passed + pairs
    group_ref[...] = groups
    first = jnp.sum(jnp.where(member, offset.astype(F32), 0.0), axis=1, keepdims=True)
    earlier = lax.broadcasted_iota(I32, (slots, slots), 1) < lax.broadcasted_iota(I32, (slots, slots), 0)
    index = jnp.sum(jnp.where((key_tall == key) & earlier, 1.0, 0.0), axis=1, keepdims=True)
    place = jnp.where(key_tall < 3 * blocks, 2.0 * first + index, -1.0)
    spare = float((blocks << 10) | (3 * blocks << 16))
    target = lax.broadcasted_iota(I32, (1, length), 1).astype(F32)
    placed = jnp.sum(jnp.where(place == target, entry_tall - spare, 0.0), axis=0, keepdims=True)
    list_ref[...] = (placed + spare).astype(I32)

    rows, parties = wanted_ref.shape
    group = hot_ref.shape[1] // rows
    half = hot_ref.shape[2] // 2 // group
    wanted = wanted_ref[...]
    member_of = lax.broadcasted_iota(I32, (rows, parties), 1) % group
    far = ((wanted >= half).astype(I32) != side_ref[0]).astype(I32)
    spot = jnp.where(wanted >= half, wanted - half, wanted) + member_of * half + far * (group * half)
    lane = lax.broadcasted_iota(I32, (rows, 2 * group * half), 1)
    for p in range(parties):
        hot = jnp.where(spot[:, p : p + 1] == lane, 1.0, 0.0)
        hot_ref[p // group, (p % group) * rows : (p % group + 1) * rows, :] = hot.astype(BF16)


def plan(count, side, places, wanted, blocks, tile):
    slots = places.shape[1]
    length = list_length(slots, blocks)
    return pl.pallas_call(
        functools.partial(plan_kernel, blocks),
        name="plan",
        in_specs=[whole(SMEM), whole(SMEM), whole(VMEM), whole(VMEM)],
        out_specs=[whole(VMEM)] * 3,
        out_shape=[
            jax.ShapeDtypeStruct((1, length), I32),
            jax.ShapeDtypeStruct((1, 128), I32),
            jax.ShapeDtypeStruct((blocks, tile, 2 * tile), BF16),
        ],
        compiler_params=params(60),
        cost_estimate=pl.CostEstimate(flops=10**7, bytes_accessed=8 << 20, transcendentals=0),
    )(count, side, places, wanted)


def unpack(entry):
    return entry & 1023, (entry >> 10) & 63, entry >> 16


def fetch_tiles(list_ref, begin, first, last, tiles_ref, store, sems):
    @pl.loop(first, last)
    def _(turn):
        for u in range(2 * PAIRS):
            tile, _, _ = unpack(list_ref[0, (begin + turn) * 2 * PAIRS + u])
            pltpu.make_async_copy(tiles_ref.at[tile], store.at[turn, u], sems.at[turn]).start()


def tile_loop(list_ref, begin, first, last, tiles_ref, store, sems, body):
    @pl.loop(first, last)
    def _(turn):
        if sems is not None:
            pltpu.make_async_copy(
                tiles_ref.at[pl.ds(0, 2 * PAIRS)], store.at[turn], sems.at[turn]
            ).wait()
        for u in range(PAIRS):
            place = (begin + turn) * 2 * PAIRS + 2 * u
            _, row, left = unpack(list_ref[0, place])
            _, _, right = unpack(list_ref[0, place + 1])
            body(store[turn, 2 * u], store[turn, 2 * u + 1], row, left, right)


def list_length(slots, blocks):
    return -(-(slots + 3 * blocks + 6 * PAIRS) // 128) * 128


def store_scratch(tiles, blocks):
    groups = (tiles.shape[0] + 3 * blocks) // (2 * PAIRS) + 4
    return [
        VMEM((groups, 2 * PAIRS) + tiles.shape[1:], BF16),
        pltpu.SemaphoreType.DMA((groups,)),
    ]


def forward_body(total, table, base):
    spare = table.shape[0] - 1

    def body(first, second, row, left, right):
        values = jnp.concatenate([first, second], axis=1)
        left = jnp.minimum(left - base, spare)
        right = jnp.minimum(right - base, spare)
        rows = jnp.concatenate([table[left], table[right]], axis=0)
        total[row] += jnp.dot(values, rows, preferred_element_type=F32)

    return body


def backward_body(spread, swapped, base):
    spare = spread.shape[0] - 1

    def body(first, second, row, left, right):
        tile = first.shape[1]
        values = jnp.concatenate([first, second], axis=1)
        product = jnp.dot(swapped[row], values, preferred_element_type=F32)
        spread[jnp.minimum(left - base, spare)] += product[:, :tile]
        spread[jnp.minimum(right - base, spare)] += product[:, tile:]

    return body


def own_forward_kernel(list_ref, group_ref, feat_ref, tiles_ref, sum_ref, table, total, store, sems):
    blocks = feat_ref.shape[0]
    begin, turns = group_ref[0, 0], group_ref[0, 3]
    fetch_tiles(list_ref, begin, 0, turns, tiles_ref, store, sems)
    total[...] = jnp.zeros_like(total)
    table[:blocks] = feat_ref[...]
    table[blocks] = jnp.zeros(table.shape[1:], BF16)
    tile_loop(list_ref, begin, 0, turns, tiles_ref, store, sems, forward_body(total, table, 0))
    sum_ref[...] = total[:blocks]


def own_forward(lists, groups, features, tiles):
    tile = tiles.shape[1]
    blocks = features.shape[0] // tile
    width = features.shape[1]
    return pl.pallas_call(
        own_forward_kernel,
        name="own_forward",
        in_specs=[whole(SMEM), whole(SMEM), whole(VMEM), whole(pltpu.HBM)],
        out_specs=whole(VMEM),
        out_shape=jax.ShapeDtypeStruct((blocks, tile, width), F32),
        scratch_shapes=[VMEM((blocks + 1, tile, width), BF16), VMEM((blocks + 1, tile, width), F32)]
        + store_scratch(tiles, blocks),
        compiler_params=params(50),
        cost_estimate=pl.CostEstimate(flops=10**9, bytes_accessed=40 << 20, transcendentals=0),
    )(lists, groups, features.reshape(blocks, tile, width), in_hbm(tiles))


def boundary_forward_kernel(
    list_ref, group_ref, near_ref, tiles_ref, sum_ref, table, total, store, sems
):
    blocks, tile, width = sum_ref.shape
    group = near_ref.shape[0] // blocks
    begin, turns = group_ref[0, 1], group_ref[0, 4]
    fetch_tiles(list_ref, begin, 0, turns, tiles_ref, store, sems)
    total[...] = jnp.zeros_like(total)
    for b in range(blocks):
        table[b] = near_ref[b * group : (b + 1) * group, 0 : tile // group, :].reshape(tile, width)
    table[blocks] = jnp.zeros(table.shape[1:], BF16)
    tile_loop(list_ref, begin, 0, turns, tiles_ref, store, sems, forward_body(total, table, blocks))
    sum_ref[...] = total[:blocks]


def boundary_forward(lists, groups, arrived, blocks, tiles):
    tile, width = tiles.shape[1], arrived.shape[2]
    return pl.pallas_call(
        boundary_forward_kernel,
        name="boundary_forward",
        in_specs=[whole(SMEM)] * 2 + [whole(VMEM), whole(pltpu.HBM)],
        out_specs=whole(VMEM),
        out_shape=jax.ShapeDtypeStruct((blocks, tile, width), F32),
        scratch_shapes=[VMEM((blocks + 1, tile, width), BF16), VMEM((blocks + 1, tile, width), F32)]
        + store_scratch(tiles, blocks),
        compiler_params=params(40),
        cost_estimate=pl.CostEstimate(flops=10**9, bytes_accessed=40 << 20, transcendentals=0),
    )(lists, groups, arrived, in_hbm(tiles))


def middle_kernel(
    list_ref, group_ref, near_ref, far_ref, hot_ref, start_ref, part_ref, weight_ref, bias_ref, cot_ref, tiles_ref,
    act_out, back_out, grads_ref, act_ref, table, total, swapped, spread, parcel, store, sems, out_sems,
):
    blocks, tile, width = act_ref.shape
    group = near_ref.shape[0] // blocks
    rows = tile // group
    weight = weight_ref[...]
    start_copy = pltpu.make_async_copy(start_ref, total.at[pl.ds(0, blocks)], out_sems.at[blocks // 2])
    start_copy.start()
    near_turns, hub_turns = group_ref[0, 4], group_ref[0, 5]
    fetch_tiles(list_ref, group_ref[0, 2], 0, hub_turns, tiles_ref, store, sems)
    fetch_tiles(list_ref, group_ref[0, 1] - hub_turns, hub_turns, hub_turns + near_turns, tiles_ref, store, sems)

    @pl.loop(0, blocks // 8)
    def _(turn):
        for i in range(8):
            b = turn * 8 + i
            near = near_ref[pl.ds(b * group, group), rows : 2 * rows, :].reshape(tile, width)
            far = far_ref[pl.ds(b * group, group), rows : 2 * rows, :].reshape(tile, width)
            picked = jnp.dot(hot_ref[b], jnp.concatenate([near, far], axis=0), preferred_element_type=F32)
            table[b] = picked.astype(BF16)

    start_copy.wait()
    total[:blocks] += part_ref[...]
    table[blocks] = jnp.zeros(table.shape[1:], BF16)
    tile_loop(
        list_ref, group_ref[0, 2], 0, hub_turns, tiles_ref, store, sems, forward_body(total, table, 2 * blocks)
    )

    @pl.loop(0, blocks // ACT)
    def _(turn):
        for i in range(ACT):
            b = turn * ACT + i
            for part in range(2):
                spread[2 * b + part] = jnp.zeros(spread.shape[1:], F32)
            preact = jnp.dot(total[b].astype(BF16), weight, preferred_element_type=F32) + bias_ref[...]
            sigmoid = 0.5 * jnp.tanh(0.5 * preact) + 0.5
            act_ref[b] = (preact * sigmoid).astype(BF16)
            slope = sigmoid * (1.0 + preact * (1.0 - sigmoid))
            upstream = (cot_ref[b].astype(F32) * slope).astype(BF16)
            swapped[b] = lax.dot_general(weight, upstream, NT, preferred_element_type=F32).astype(BF16)

    results = (
        pltpu.make_async_copy(act_ref, act_out, out_sems.at[blocks // 2]),
        pltpu.make_async_copy(swapped.at[pl.ds(0, blocks)], back_out, out_sems.at[blocks // 2 + 1]),
    )
    for result in results:
        result.start()
    spread[2 * blocks] = jnp.zeros(spread.shape[1:], F32)
    add = backward_body(spread, swapped, blocks)
    tile_loop(list_ref, group_ref[0, 2], 0, hub_turns, tiles_ref, store, None, add)
    tile_loop(
        list_ref, group_ref[0, 1] - hub_turns, hub_turns, hub_turns + near_turns, tiles_ref, store, sems, add
    )

    chunk = 2 * group

    def send(turn):
        return pltpu.make_async_copy(
            parcel.at[pl.ds(turn * chunk, chunk)], grads_ref.at[pl.ds(turn * chunk, chunk)], out_sems.at[turn]
        )

    @pl.loop(0, blocks // 2)
    def _(turn):
        for i in range(2):
            b = turn * 2 + i
            for part in range(2):
                out = jnp.transpose(spread[part * blocks + b].astype(BF16))
                parcel[pl.ds(b * group, group), part * rows : (part + 1) * rows, :] = out.reshape(
                    group, rows, width
                )
        send(turn).start()

    @pl.loop(0, blocks // 2)
    def _(turn):
        send(turn).wait()

    for result in results:
        result.wait()


def middle(lists, groups, arrived, other, hot, start, near, weight, bias, cotangent, tiles):
    blocks, tile, width = start.shape
    parties = arrived.shape[0]
    rows = blocks * tile // parties
    return pl.pallas_call(
        middle_kernel,
        name="middle",
        in_specs=[whole(SMEM)] * 2
        + [whole(VMEM)] * 3
        + [whole(pltpu.HBM)]
        + [whole(VMEM)] * 4
        + [whole(pltpu.HBM)],
        out_specs=[whole(pltpu.HBM)] * 3,
        out_shape=[
            pltpu.HBM((blocks, tile, width), BF16),
            pltpu.HBM((blocks, width, tile), BF16),
            pltpu.HBM((parties, 2 * rows, width), BF16),
        ],
        scratch_shapes=[
            VMEM((blocks, tile, width), BF16),
            VMEM((blocks + 1, tile, width), BF16),
            VMEM((blocks + 1, tile, width), F32),
            VMEM((blocks + 1, width, tile), BF16),
            VMEM((2 * blocks + 1, width, tile), F32),
            VMEM((parties, 2 * rows, width), BF16),
        ]
        + store_scratch(tiles, blocks)
        + [pltpu.SemaphoreType.DMA((blocks // 2 + 2,))],
        compiler_params=params(42),
        cost_estimate=pl.CostEstimate(flops=4 * 10**9, bytes_accessed=60 << 20, transcendentals=10**6),
    )(
        lists, groups, arrived, other, hot, in_hbm(start), near, weight, bias, cotangent.reshape(blocks, tile, width), in_hbm(tiles)
    )


def own_backward_kernel(
    list_ref, group_ref, back_ref, names_ref, tiles_ref, own_ref, hot_ref, swapped, spread, store, sems, back_sem
):
    blocks = back_ref.shape[0]
    begin, turns = group_ref[0, 0], group_ref[0, 3]
    back_copy = pltpu.make_async_copy(back_ref, swapped.at[pl.ds(0, blocks)], back_sem)
    back_copy.start()
    fetch_tiles(list_ref, begin, 0, turns, tiles_ref, store, sems)
    spread[...] = jnp.zeros_like(spread)
    back_copy.wait()
    tile_loop(list_ref, begin, 0, turns, tiles_ref, store, sems, backward_body(spread, swapped, 0))

    @pl.loop(0, blocks // 2)
    def _(turn):
        for i in range(2):
            own_ref[turn * 2 + i] = jnp.transpose(spread[turn * 2 + i])

    parties, total, width = names_ref.shape
    group = parties // blocks
    rows = width // group
    names = names_ref[:, total - 8, :].astype(F32)
    party = lax.broadcasted_iota(I32, names.shape, 0)
    lane = lax.broadcasted_iota(I32, names.shape, 1)
    names = jnp.where(lane // rows == party % group, names, 0.0).astype(BF16)
    block = lax.broadcasted_iota(I32, (blocks, parties), 0)
    gather = jnp.where(lax.broadcasted_iota(I32, (blocks, parties), 1) // group == block, 1.0, 0.0)
    lines = jnp.dot(gather.astype(BF16), names, preferred_element_type=F32)
    hub = lax.broadcasted_iota(I32, hot_ref.shape[1:], 0).astype(F32)
    for b in range(blocks):
        hot_ref[b] = jnp.where(hub == lines[b : b + 1, :], 1.0, 0.0).astype(BF16)


def own_backward(lists, groups, back, arrived, tiles, hubs):
    blocks, width, tile = back.shape
    return pl.pallas_call(
        own_backward_kernel,
        name="own_backward",
        in_specs=[whole(SMEM)] * 2 + [whole(pltpu.HBM), whole(VMEM), whole(pltpu.HBM)],
        out_specs=[whole(VMEM)] * 2,
        out_shape=[
            jax.ShapeDtypeStruct((blocks, tile, width), F32),
            jax.ShapeDtypeStruct((blocks, hubs, width), BF16),
        ],
        scratch_shapes=[VMEM((blocks + 1, width, tile), BF16), VMEM((blocks + 1, width, tile), F32)]
        + store_scratch(tiles, blocks)
        + [pltpu.SemaphoreType.DMA],
        compiler_params=params(50),
        cost_estimate=pl.CostEstimate(flops=10**9, bytes_accessed=40 << 20, transcendentals=0),
    )(lists, groups, in_hbm(back), arrived, in_hbm(tiles))


def returned_kernel(send_ref, own_ref, back_ref, hot_ref, sal_out, hub_ref, stage, hot, first, chains, sems):
    rows, parties = send_ref.shape
    blocks, _, width = hot_ref.shape
    group = parties // blocks
    own_copy = pltpu.make_async_copy(own_ref, first, sems.at[0])
    hot_copy = pltpu.make_async_copy(hot_ref, hot, sems.at[1])
    own_copy.start()
    hot_copy.start()
    for chain in chains:
        chain[...] = jnp.zeros_like(chain)

    @pl.loop(0, parties // 4)
    def _(turn):
        for i in range(4):
            stage[turn * 4 + i] = back_ref[turn * 4 + i, 0:rows, :].astype(F32)

    own_copy.wait()
    sums = (first,) + tuple(chains)

    @pl.loop(0, rows)
    def _(j):
        for q in range(parties):
            chain = sums[q % len(sums)]
            row = send_ref[j, q]
            chain[pl.ds(row, 1), :] += stage[q, pl.ds(j, 1), :]

    turns = sems.shape[0] - 2
    size = first.shape[0] // turns

    def result(turn):
        part = pl.ds(turn * size, size)
        return pltpu.make_async_copy(first.at[part], sal_out.at[part], sems.at[turn + 2])

    @pl.loop(0, turns)
    def _(turn):
        part = pl.ds(turn * size, size)
        total = first[part, :]
        for chain in chains:
            total = total + chain[part, :]
        first[part, :] = total
        result(turn).start()

    hot_copy.wait()
    total = jnp.zeros(hub_ref.shape, F32)
    for b in range(0, blocks, 2):
        grads = back_ref[b * group : (b + 2) * group, rows:, :].reshape(2 * group * rows, width)
        pair = jnp.concatenate([hot[b], hot[b + 1]], axis=1)
        total += jnp.dot(pair, grads, preferred_element_type=F32)
    hub_ref[...] = total

    @pl.loop(0, turns)
    def _(turn):
        result(turn).wait()


def returned_rows(send, own, returned, hot):
    rows, parties = send.shape
    own_rows, width = own.shape
    return pl.pallas_call(
        returned_kernel,
        name="returned_rows",
        in_specs=[whole(SMEM), whole(pltpu.HBM), whole(VMEM), whole(pltpu.HBM)],
        out_specs=[whole(pltpu.HBM), whole(VMEM)],
        out_shape=[
            pltpu.HBM((own_rows, width), F32),
            jax.ShapeDtypeStruct((hot.shape[1], width), F32),
        ],
        scratch_shapes=[
            VMEM((parties, rows, width), F32),
            VMEM(hot.shape, BF16),
            VMEM((own_rows, width), F32),
            [VMEM((own_rows, width), F32)] * (CHAINS - 1),
            pltpu.SemaphoreType.DMA((2 + TURNS,)),
        ],
        compiler_params=params(32),
        cost_estimate=pl.CostEstimate(flops=10**8, bytes_accessed=40 << 20, transcendentals=0),
    )(send, in_hbm(own), returned, in_hbm(hot))


def body(
    features, hubs, weight, bias, cotangent, tiles, tile_blocks, tile_count, halo_send, replica_rows
):
    own_rows, width = features.shape
    tile = tiles.shape[1]
    blocks = own_rows // tile
    send = halo_send[0].T
    wanted = replica_rows[0].T
    parties = send.shape[1]
    side = (lax.axis_index("dom") % 2).astype(I32).reshape(1)

    pairs = [(i, i ^ 1) for i in range(parties)]

    outgoing = outgoing_rows(send, features, hubs, wanted)
    arrived = lax.all_to_all(outgoing, "dom", split_axis=0, concat_axis=0, tiled=True)
    lists, groups, hot = plan(tile_count, side, tile_blocks.T, wanted, blocks, tile)
    start = own_forward(lists, groups, features, tiles)
    other = lax.ppermute(arrived, "dom", pairs)
    near = boundary_forward(lists, groups, arrived, blocks, tiles)
    act, back, grads = middle(
        lists, groups, arrived, other, hot, start, near, weight, bias.reshape(1, -1), cotangent, tiles
    )
    returned = lax.all_to_all(grads, "dom", split_axis=0, concat_axis=0, tiled=True)
    own, hub_hot = own_backward(lists, groups, back, arrived, tiles, hubs.shape[0])
    saliency, hub_saliency = returned_rows(send, own.reshape(own_rows, width), returned, hub_hot)
    return act.reshape(own_rows, width), saliency, hub_saliency


def solution(mesh):
    placed = (
        P("dom", None),
        P("dom", None),
        P(),
        P(),
        P("dom", None),
        P("dom", None, None),
        P("dom", None),
        P("dom"),
        P("dom", None, None),
        P("dom", None, None),
    )
    return jax.shard_map(
        body,
        mesh=mesh,
        in_specs=placed,
        out_specs=(P("dom", None), P("dom", None), P("dom", None)),
        check_vma=False,
    )
```
